768 devices in a mesh: lon: 24 (over x_lo, z), lat: 32 (over x_hi, y, core).
Axes of the slice: x: 4 (x_hi: 2, x_lo: 2; x = x_hi * 2 + x_lo), y: 8, z: 12, core: 2. Of those that a mesh axis runs over, the one named last changes fastest.
Arguments:
- free_elevation: float32 [512, 6144], P('lat', 'lon'), may hold values from -3 to 3
- zonal_volume_carriage: float32 [512, 6144], P('lat', 'lon'), may hold values from -2 to 2
- meridional_volume_carriage: float32 [512, 6144], P('lat', 'lon'), may hold values from -2 to 2
- thermal_field: float32 [60, 512, 6144], P(None, 'lat', 'lon'), may hold values from -6 to 6
- flooded_strata_number: int32 [512, 6144], P('lat', 'lon'), may hold values from 0 to 60, as said below
- aerial_exchanges: float32 [5, 256, 3072], P(None, 'lat', 'lon'), may hold values from -6 to 6
- aerial_terrain_flags: int32 [256, 3072], P('lat', 'lon'), may hold values 0 or 1
- donor_tile_number: int32 [4, 512, 48], P(None, 'lat', 'lon'), may hold values from 0 to 23
- donor_point_number: int32 [4, 512, 6144], P(None, 'lat', 'lon'), may hold values from 0 to 127
- pairing_coefficients: float32 [4, 512, 6144], P(None, 'lat', 'lon'), may hold values from 0 to 0.5
Outputs:
- advanced_elevation: float32 [512, 6144], P('lat', 'lon')
- transport_x_next: float32 [512, 6144], P('lat', 'lon')
- transport_y_next: float32 [512, 6144], P('lat', 'lon')
- advanced_thermal_field: float32 [60, 512, 6144], P(None, 'lat', 'lon')
- marine_skin_condition: float32 [4, 256, 3072], P(None, 'lat', 'lon')
The draws below stay inside these ranges and needn't reach their ends.
Inputs may be any that keep to these rules, and one draw needn't show every extreme that they name: flooded_strata_number is 0 on land; wet columns hold 1 to 60 levels. donor_tile_number // 8 - 1 is the source tile's offset in latitude and donor_tile_number mod 8 the source block (row) within it; the longitude tile is the target's.
All inputs are finite; a program needn't handle non-finite values. No bound on the sum of `aerial_terrain_flags` on one device may be relied on, other than what follows from the above.
Results may differ from the reference program's by a relative error of at most 0.0003.
Values sent between devices are 32-bit elements; how exact they have to be, the bound alone decides.
A program may use at most 32 MiB of HBM per device.

```python
import math
import jax
import jax.numpy as jnp
from jax import lax

ALAT = 8
ALON = 128
MARINE_STRATA = 60
SUBS = 3
INTERSECTIONS = 4
NFLUX = 5
NSURF = 4
OLAT = 16
OLON = 256
ALAT_ALL = 256
ALON_ALL = 3072
MARINE_LATITUDES = 512
MARINE_LONGITUDES = 6144
N_LON = 24


def draw_flooded_strata_number(key, part):
    depth_key = jax.random.fold_in(key, 11)
    land_key = jax.random.fold_in(key, 23)
    grid_shape = (MARINE_LATITUDES, MARINE_LONGITUDES)
    levels_drawn = jax.random.randint(depth_key, grid_shape, 1, MARINE_STRATA + 1)
    row_ids = lax.broadcasted_iota(jnp.int32, grid_shape, 0)
    column_ids = lax.broadcasted_iota(jnp.int32, grid_shape, 1)
    land_share = (row_ids // 4 * 3 + column_ids // 16 * 5) % 8
    rolled = jax.random.randint(land_key, grid_shape, 0, 10)
    return jnp.where(rolled < land_share, 0, levels_drawn).astype(jnp.int32)


def place_ends(entries, rng, smallest, high):
    index_at = [jax.random.randint(jax.random.fold_in(rng, axis), (), 0, length) for axis, length in enumerate(entries.shape)]
    widest = entries.shape.index(max(entries.shape))
    beside = index_at[:widest] + [(index_at[widest] + 1) % entries.shape[widest]] + index_at[widest + 1:]
    return entries.at[tuple(index_at)].set(smallest).at[tuple(beside)].set(high)


def block_levels(own_key, shape, split, least, top_value):
    gain = 1.0
    for dim, parts in split:
        draws = jax.random.uniform(jax.random.fold_in(jax.random.fold_in(own_key, 6), dim), (parts,), jnp.float32, least / len(split), top_value / len(split))
        gain = gain * jnp.repeat(jnp.exp(draws), shape[dim] // parts).reshape((-1,) + (1,) * (len(shape) - 1 - dim))
    return gain


def gaussian(key, shape, scale, bound, cuts=(), kind=jnp.bfloat16):
    result = scale * jax.random.normal(key, shape, jnp.float32)
    if cuts:
        result = result * block_levels(key, shape, cuts, -0.22, 0.18)
    return jnp.clip(result, -bound, bound).astype(kind)


def setup_inputs(seed: int = 0) -> dict:
    keys = jax.random.split(jax.random.key(seed), 11)
    return {
        "free_elevation": gaussian(keys[0], (MARINE_LATITUDES, MARINE_LONGITUDES), 0.5, 3.0, ((0, 32), (1, 24)), jnp.float32),
        "zonal_volume_carriage": gaussian(keys[1], (MARINE_LATITUDES, MARINE_LONGITUDES), 0.3, 2.0, ((0, 32), (1, 24)), jnp.float32),
        "meridional_volume_carriage": gaussian(keys[2], (MARINE_LATITUDES, MARINE_LONGITUDES), 0.3, 2.0, ((0, 32), (1, 24)), jnp.float32),
        "thermal_field": gaussian(keys[3], (MARINE_STRATA, MARINE_LATITUDES, MARINE_LONGITUDES), 1.0, 6.0, ((1, 32), (2, 24)), jnp.float32),
        "flooded_strata_number": draw_flooded_strata_number(jax.random.fold_in(keys[10], 71), 0),
        "aerial_exchanges": gaussian(keys[5], (NFLUX, ALAT_ALL, ALON_ALL), 1.0, 6.0, ((1, 32), (2, 24)), jnp.float32),
        "aerial_terrain_flags": place_ends((jax.random.randint(keys[6], (ALAT_ALL, ALON_ALL), 0, 10) < 3).astype(jnp.int32), jax.random.fold_in(keys[6], 1), 0, 1),
        "donor_tile_number": place_ends(jax.random.randint(keys[7], (INTERSECTIONS, MARINE_LATITUDES, 2 * N_LON), 0, 3 * ALAT), jax.random.fold_in(keys[7], 1), 0, (3 * ALAT) - 1).astype(jnp.int32),
        "donor_point_number": place_ends(jax.random.randint(keys[8], (INTERSECTIONS, MARINE_LATITUDES, MARINE_LONGITUDES), 0, ALON), jax.random.fold_in(keys[8], 1), 0, ALON - 1).astype(jnp.int32),
        "pairing_coefficients": jnp.clip(0.5 * jax.random.uniform(keys[9], (INTERSECTIONS, MARINE_LATITUDES, MARINE_LONGITUDES), jnp.float32) ** block_levels(keys[9], (INTERSECTIONS, MARINE_LATITUDES, MARINE_LONGITUDES), ((1, 32), (2, 24)), -0.2, 0.2), 0.0, 0.5),
    }


grav_step = 0.6
height_step = 0.6
wind_step = 0.5
fresh_step = 0.5
mixing_fourth = 0.02
advect_coef = 0.1
diapycnal_diffusion = 0.2
heat_gain = 0.3
light_gain = 0.3
light_decay = 8.0
depth_floor = 0.25
area_floor = 1.0


def column_depth(stratum_tally_sheet, stratum_entries):
    def add_level(level_index, running):
        level_value = jnp.asarray(level_index).astype(jnp.float32)
        thickness = (1.0 + 2.0 * level_value / stratum_entries) / (2.0 * stratum_entries)
        return running + jnp.where(level_value < stratum_tally_sheet, thickness, 0.0)
    return lax.fori_loop(0, stratum_entries, add_level, jnp.zeros_like(stratum_tally_sheet))


def barotropic_step(planes, stratum_entries):
    height = planes[0]
    zonal_velocity = planes[1]
    meridional_velocity = planes[2]
    stratum_tally_sheet = planes[3]
    wind_east = planes[4]
    wind_north = planes[5]
    fresh_water = planes[6]
    stratum_thicknesses = column_depth(stratum_tally_sheet, stratum_entries)
    lone_flooded_point = (stratum_tally_sheet > 0.5).astype(jnp.float32)
    east_face = lone_flooded_point[1:-1, :-1] * lone_flooded_point[1:-1, 1:]
    east_depth = jnp.minimum(stratum_thicknesses[1:-1, :-1], stratum_thicknesses[1:-1, 1:])
    east_flow = east_face * (zonal_velocity[1:-1, :-1] - grav_step * east_depth * (height[1:-1, 1:] - height[1:-1, :-1]) + wind_step * wind_east[1:-1, :-1])
    north_face = lone_flooded_point[:-1, 1:-1] * lone_flooded_point[1:, 1:-1]
    north_depth = jnp.minimum(stratum_thicknesses[:-1, 1:-1], stratum_thicknesses[1:, 1:-1])
    north_flow = north_face * (meridional_velocity[:-1, 1:-1] - grav_step * north_depth * (height[1:, 1:-1] - height[:-1, 1:-1]) + wind_step * wind_north[:-1, 1:-1])
    spread = east_flow[:, 1:] - east_flow[:, :-1] + north_flow[1:, :] - north_flow[:-1, :]
    inner_wet = lone_flooded_point[1:-1, 1:-1]
    new_height = height[1:-1, 1:-1] + inner_wet * (fresh_step * fresh_water[1:-1, 1:-1] - height_step * spread)
    return jnp.stack([new_height, east_flow[:, 1:], north_flow[1:, :], stratum_tally_sheet[1:-1, 1:-1],
                      wind_east[1:-1, 1:-1], wind_north[1:-1, 1:-1], fresh_water[1:-1, 1:-1]])


def face_masks(count_border, level_order):
    east_open = (level_order < jnp.minimum(count_border[:, :-1], count_border[:, 1:])).astype(jnp.float32)
    north_open = (level_order < jnp.minimum(count_border[:-1, :], count_border[1:, :])).astype(jnp.float32)
    return east_open, north_open


def laplace(field, count_border, level_order):
    east_open, north_open = face_masks(count_border, level_order)
    flux_east = east_open * (field[..., 1:] - field[..., :-1])
    flux_north = north_open * (field[..., 1:, :] - field[..., :-1, :])
    return (flux_east[..., 1:-1, 1:] - flux_east[..., 1:-1, :-1]
            + flux_north[..., 1:, 1:-1] - flux_north[..., :-1, 1:-1])


def face_speeds(count_border, east_border, north_border, stratum_entries):
    stratum_thicknesses = column_depth(count_border, stratum_entries)
    speed_east = east_border[:, :-1] / jnp.maximum(jnp.minimum(stratum_thicknesses[:, :-1], stratum_thicknesses[:, 1:]), depth_floor)
    speed_north = north_border[:-1, :] / jnp.maximum(jnp.minimum(stratum_thicknesses[:-1, :], stratum_thicknesses[1:, :]), depth_floor)
    return speed_east, speed_north


def horizontal_tendency(temp_border, lap_border, count_border, speed_east, speed_north, level_order):
    mixing = laplace(lap_border, count_border, level_order)
    east_open, north_open = face_masks(count_border, level_order)
    carry_east = east_open * speed_east * 0.5 * (temp_border[..., 1:] + temp_border[..., :-1])
    carry_north = north_open * speed_north * 0.5 * (temp_border[..., 1:, :] + temp_border[..., :-1, :])
    advect = (carry_east[..., 1:-1, 1:] - carry_east[..., 1:-1, :-1]
              + carry_north[..., 1:, 1:-1] - carry_north[..., :-1, 1:-1])
    return -advect_coef * advect - mixing_fourth * mixing


def profile_change_rate(thermal_field, lateral_contribution, stratum_tally_sheet, boundary_thermal_exchange, solar_radiation, stratum_entries):
    level_order = jnp.arange(stratum_entries, dtype=jnp.float32)[:, None, None]
    flooded_point_flags = (level_order < stratum_tally_sheet).astype(jnp.float32)
    beneath_stratum_flooded = (level_order + 1.0 < stratum_tally_sheet).astype(jnp.float32)
    sinking_exchange = beneath_stratum_flooded[:-1] * (thermal_field[1:] - thermal_field[:-1])
    blank_sheet = jnp.zeros_like(thermal_field[:1])
    radial_contribution = jnp.concatenate([sinking_exchange, blank_sheet]) - jnp.concatenate([blank_sheet, sinking_exchange])
    absorb = jnp.exp(-level_order / light_decay) * (1.0 - math.exp(-1.0 / light_decay))
    top_level = (level_order < 0.5).astype(jnp.float32)
    donor_entries = light_gain * absorb * solar_radiation + heat_gain * boundary_thermal_exchange * top_level
    return thermal_field + flooded_point_flags * (diapycnal_diffusion * radial_contribution + lateral_contribution + donor_entries)


def gather_forcing(flux_table, flat_index, weight):
    running = jnp.zeros((flux_table.shape[0],) + flat_index.shape[1:], jnp.float32)
    for link_index in range(flat_index.shape[0]):
        running = running + jnp.take(flux_table, flat_index[link_index], axis=1) * weight[link_index][None]
    return running


def spread_back(uppermost_stratum, lone_flooded_point, flat_index, weight, segments):
    link_share = weight * lone_flooded_point[None]
    flat_cells = flat_index.reshape(-1)

    def scatter_plane(plane):
        return jax.ops.segment_sum((plane[None] * link_share).reshape(-1), flat_cells, num_segments=segments)

    link_sums = jnp.stack([scatter_plane(uppermost_stratum[plane_index]) for plane_index in range(uppermost_stratum.shape[0])])
    link_area = jax.ops.segment_sum(link_share.reshape(-1), flat_cells, num_segments=segments)
    return link_sums, link_area


def haloed_sphere(field, width):
    wrapped = jnp.concatenate([field[..., -width:], field, field[..., :width]], axis=-1)
    widths = [(0, 0)] * (field.ndim - 2) + [(width, width), (0, 0)]
    return jnp.pad(wrapped, widths)


def reference(free_elevation, zonal_volume_carriage, meridional_volume_carriage, thermal_field, flooded_strata_number, aerial_exchanges, aerial_terrain_flags,
              donor_tile_number, donor_point_number, pairing_coefficients):
    open_sea = (1 - aerial_terrain_flags).astype(jnp.float32)
    masked = aerial_exchanges * open_sea[None]
    padded = jnp.pad(masked, ((0, 0), (ALAT, ALAT), (0, 0)))
    flux_table = padded.reshape(NFLUX, -1)
    row_ids = lax.broadcasted_iota(jnp.int32, (MARINE_LATITUDES, MARINE_LONGITUDES), 0)
    column_ids = lax.broadcasted_iota(jnp.int32, (MARINE_LATITUDES, MARINE_LONGITUDES), 1)
    block_row = jnp.repeat(donor_tile_number, ALON, axis=2)
    global_row = (row_ids // OLAT) * ALAT + block_row
    global_column = (column_ids // OLON) * ALON + donor_point_number
    flat_index = (global_row * ALON_ALL + global_column).astype(jnp.int32)
    boundary_driving = gather_forcing(flux_table, flat_index, pairing_coefficients)

    stratum_tally_sheet = flooded_strata_number.astype(jnp.float32)
    present_scalar_field = jnp.stack([free_elevation, zonal_volume_carriage, meridional_volume_carriage, stratum_tally_sheet, boundary_driving[0], boundary_driving[1], boundary_driving[4]])
    for cycle_index in range(SUBS):
        present_scalar_field = barotropic_step(haloed_sphere(present_scalar_field, 1), MARINE_STRATA)
    advanced_elevation = present_scalar_field[0]
    zonal_velocity = present_scalar_field[1]
    meridional_velocity = present_scalar_field[2]

    thermal_field_haloed = haloed_sphere(thermal_field, 2)
    count_wide = haloed_sphere(stratum_tally_sheet, 2)
    count_border = count_wide[1:-1, 1:-1]
    flows = haloed_sphere(present_scalar_field[1:3], 1)
    speed_east, speed_north = face_speeds(count_border, flows[0], flows[1], MARINE_STRATA)

    def by_stratum(level_args):
        temp_level, level_order = level_args
        lap_border = laplace(temp_level, count_wide, level_order)
        return horizontal_tendency(temp_level[1:-1, 1:-1], lap_border, count_border, speed_east, speed_north, level_order)

    lateral_contribution = lax.map(by_stratum, (thermal_field_haloed, jnp.arange(MARINE_STRATA, dtype=jnp.float32)))
    advanced_thermal_field = profile_change_rate(thermal_field, lateral_contribution, stratum_tally_sheet, boundary_driving[2], boundary_driving[3], MARINE_STRATA)

    lone_flooded_point = (stratum_tally_sheet > 0.5).astype(jnp.float32)
    stratum_thicknesses = jnp.maximum(column_depth(stratum_tally_sheet, MARINE_STRATA), depth_floor)
    uppermost_stratum = jnp.stack([advanced_thermal_field[0], advanced_elevation, zonal_velocity / stratum_thicknesses, meridional_velocity / stratum_thicknesses]) * lone_flooded_point[None]
    segments = (ALAT_ALL + 2 * ALAT) * ALON_ALL
    link_sums, link_area = spread_back(uppermost_stratum, lone_flooded_point, flat_index, pairing_coefficients, segments)
    link_sums = link_sums.reshape(NSURF, ALAT_ALL + 2 * ALAT, ALON_ALL)[:, ALAT:ALAT + ALAT_ALL]
    link_area = link_area.reshape(ALAT_ALL + 2 * ALAT, ALON_ALL)[ALAT:ALAT + ALAT_ALL]
    marine_skin_condition = open_sea[None] * link_sums / jnp.maximum(link_area, area_floor)[None]
    return advanced_elevation, zonal_velocity, meridional_velocity, advanced_thermal_field, marine_skin_condition
```

```python
import math

import jax
import jax.numpy as jnp
from jax import lax
from jax.experimental import pallas as pl
from jax.experimental.pallas import tpu as pltpu
from jax.sharding import PartitionSpec as P

SUBS = 3
grav_step = 0.6
height_step = 0.6
wind_step = 0.5
fresh_step = 0.5
mixing_fourth = 0.02
advect_coef = 0.1
diapycnal_diffusion = 0.2
heat_gain = 0.3
light_gain = 0.3
light_decay = 8.0
depth_floor = 0.25
area_floor = 1.0

f32 = jnp.float32
bf16 = jnp.bfloat16

FLUX_ORDER = (0, 1, 4, 2, 3)


def lanes(shape):
    return lax.broadcasted_iota(jnp.int32, shape, len(shape) - 1)


def subs(shape):
    return lax.broadcasted_iota(jnp.int32, shape, len(shape) - 2)


def roll(x, shift, axis):
    return pltpu.roll(x, shift % x.shape[axis], axis)


def east(x):
    return roll(x, -1, 1)


def west(x):
    return roll(x, 1, 1)


def north(x):
    return roll(x, -1, 0)


def south(x):
    return roll(x, 1, 0)


def put(ref, value):
    for b in range(3):
        ref[b] = value[:, b * 128:b * 128 + 128]


def whole(ref):
    return jnp.concatenate([ref[b] for b in range(3)], axis=1)


def own_part(ref):
    return jnp.concatenate([ref[b, 0:16] for b in range(2)], axis=1)


def kernel(
    h_in, u_in, v_in, t_in, n_in, x_in, flag_in, tile, pt_in, w_in,
    o_height, o_zonal, o_meridional, tnew, o_skin,
    planes, count_int, tn, flux, flags, pt, wt,
    rows_in, rows_wide, masked, rx, col_e, col_w, rcol_e, rcol_w, rdiag, rns,
    tv, tpack, rt_e, rt_w, rt_diag,
    forcing, fcol_e, fcol_w, rf_e, rf_w, rf_diag, rf_ns,
    cnt_r, me_r, mn_r, se_r, sn_r,
    lap, mix, tpart, flow, rowcol, row_hot, sv, cells, table, rtable, top_part,
    in_sem, send_sem, recv_sem,
):
    strata = t_in.shape[0] // 16
    n_lon, n_lat = lax.axis_size("lon"), lax.axis_size("lat")
    lon, lat = lax.axis_index("lon"), lax.axis_index("lat")
    le, lw = lax.rem(lon + 1, n_lon), lax.rem(lon + n_lon - 1, n_lon)
    ln, ls = lax.rem(lat + 1, n_lat), lax.rem(lat + n_lat - 1, n_lat)
    to_n, to_s = {"lon": lon, "lat": ln}, {"lon": lon, "lat": ls}
    to_e, to_w = {"lon": le, "lat": lat}, {"lon": lw, "lat": lat}
    to_ne, to_nw = {"lon": le, "lat": ln}, {"lon": lw, "lat": ln}
    to_se, to_sw = {"lon": le, "lat": ls}, {"lon": lw, "lat": ls}

    loads = [
        (x_in, flux), (flag_in, flags), (n_in, count_int), (h_in, planes.at[0]), (u_in, planes.at[1]),
        (v_in, planes.at[2]), (t_in.at[pl.ds(0, 16)], planes.at[4]),
        (pt_in.at[:, pl.ds(0, 128)], pt.at[0]), (pt_in.at[:, pl.ds(128, 128)], pt.at[1]),
        (w_in.at[:, pl.ds(0, 128)], wt.at[0]), (w_in.at[:, pl.ds(128, 128)], wt.at[1]),
        (tile, rows_in), (t_in.at[:, pl.ds(0, 128)], tn.at[0, pl.ds(0, strata * 16)]),
        (t_in.at[:, pl.ds(128, 128)], tn.at[1, pl.ds(0, strata * 16)]),
    ]
    load = [pltpu.make_async_copy(a, b, in_sem.at[i]) for i, (a, b) in enumerate(loads)]
    for c in load:
        c.start()

    barrier = pltpu.get_barrier_semaphore()
    for where in (to_n, to_s, to_e, to_w, to_ne, to_nw, to_se, to_sw):
        pl.semaphore_signal(barrier, inc=1, device_id=where, device_id_type=pl.DeviceIdType.MESH)

    sends = []

    def send(src, dst, where):
        i = len(sends)
        c = pltpu.make_async_remote_copy(
            src_ref=src, dst_ref=dst, send_sem=send_sem.at[i], recv_sem=recv_sem.at[i],
            device_id=where, device_id_type=pl.DeviceIdType.MESH,
        )
        c.start()
        sends.append(c)
        return c

    lane = lanes((8, 128))
    sub = subs((8, 128))

    load[0].wait()
    load[1].wait()
    open_sea = (1 - flags[...]).astype(f32)
    for f, g in enumerate(FLUX_ORDER):
        masked[f * 8:f * 8 + 8] = flux[g * 8:g * 8 + 8] * open_sea
    for i in range(2, 7):
        load[i].wait()
    planes[3] = count_int[...].astype(f32)

    def pack_columns(tiles, n, dst_e, dst_w):
        for rt in range(2):
            pe = pw = jnp.zeros((8, 128), f32)
            for p in range(n):
                here = (lane >= 3 * p) & (lane < 3 * p + 3)
                pe = jnp.where(here, roll(tiles(p, rt, 1), 3 * p - 125, 1), pe)
                pw = jnp.where(here, roll(tiles(p, rt, 0), 3 * p, 1), pw)
            dst_e[rt * 8:rt * 8 + 8] = pe
            dst_w[rt * 8:rt * 8 + 8] = pw

    def plane_tile(p, rt, b):
        return planes[p, rt * 8:rt * 8 + 8, b * 128:b * 128 + 128]

    pack_columns(plane_tile, 5, col_e, col_w)

    pl.semaphore_wait(barrier, 8)

    x_n = send(masked, rx.at[0], to_n)
    x_s = send(masked, rx.at[1], to_s)
    p_copies = [
        send(col_e, rcol_w, to_e),
        send(col_w, rcol_e, to_w),
        send(col_e.at[pl.ds(8, 8)], rdiag.at[3], to_ne),
        send(col_w.at[pl.ds(8, 8)], rdiag.at[2], to_nw),
        send(col_e.at[pl.ds(0, 8)], rdiag.at[1], to_se),
        send(col_w.at[pl.ds(0, 8)], rdiag.at[0], to_sw),
        send(planes.at[:, pl.ds(8, 8)], rns.at[1], to_n),
        send(planes.at[:, pl.ds(0, 8)], rns.at[0], to_s),
    ]

    load[11].wait()
    for j in range(8):
        rows_wide[j:j + 1, 0:16] = rows_in[j // 2, j % 2:j % 2 + 1, :].astype(f32)
    row_of = jnp.zeros((8, 128), f32)
    for j in range(8):
        here = lax.shift_right_logical(lane, 4) == j
        row_of = jnp.where(here, roll(jnp.broadcast_to(rows_wide[j:j + 1, :], (8, 128)), 16 * j, 1), row_of)
    row_id = subs((128, 128))
    hot = (row_id & 31).astype(f32) == jnp.concatenate([row_of] * 16, axis=0)
    hot = jnp.where(hot & (row_id < 96), 1.0, 0.0)
    row_hot[...] = hot[0:32].astype(bf16)
    rowcol[...] = jnp.transpose(hot).astype(bf16)

    load[12].wait()
    load[13].wait()
    pad = 64 * 16 - strata * 16
    for b in range(2):
        tn[b, strata * 16:] = jnp.zeros((pad, 128), f32)

    half = lax.shift_right_logical(lane, 1)

    def turn(r, carry):
        carry = list(carry)
        for q in range(8):
            g, q4 = q // 4, q % 4
            here = half == r + 16 * q4
            t0 = tn[0, pl.ds(q * 128 + r, 8, stride=16), :]
            t1 = tn[1, pl.ds(q * 128 + r, 8, stride=16), :]
            tv[r, q * 8:q * 8 + 8, 0:128] = t0
            tv[r, q * 8:q * 8 + 8, 128:256] = t1
            at = 2 * r + 32 * q4
            carry[g] = jnp.where(here, pltpu.roll(t1, lax.rem(at + 2, 128), 1), carry[g])
            carry[2 + g] = jnp.where(here, pltpu.roll(t0, at, 1), carry[2 + g])
        return tuple(carry)

    packs = lax.fori_loop(0, 16, turn, (jnp.zeros((8, 128), f32),) * 4, unroll=4)
    for i in range(4):
        tpack[i // 2, (i % 2) * 8:(i % 2) * 8 + 8] = packs[i]

    t_copies = [
        send(tpack.at[0], rt_w, to_e),
        send(tpack.at[1], rt_e, to_w),
        send(tpack.at[0], rt_diag.at[3], to_ne),
        send(tpack.at[1], rt_diag.at[2], to_nw),
        send(tpack.at[0], rt_diag.at[1], to_se),
        send(tpack.at[1], rt_diag.at[0], to_sw),
        send(tv.at[pl.ds(14, 2), :, pl.ds(0, 256)], tv.at[pl.ds(22, 2), :, pl.ds(0, 256)], to_n),
        send(tv.at[pl.ds(0, 2), :, pl.ds(0, 256)], tv.at[pl.ds(16, 2), :, pl.ds(0, 256)], to_s),
    ]

    for i in range(7, 11):
        load[i].wait()

    x_n.wait_recv()
    x_s.wait_recv()
    keep_south = jnp.broadcast_to(lat, (8, 128)) > 0
    keep_north = jnp.broadcast_to(lat, (8, 128)) < n_lat - 1
    zero = jnp.zeros((8, 128), f32)
    for f in range(5):
        part = slice(f * 8, f * 8 + 8)
        bands = jnp.concatenate(
            [jnp.where(keep_south, rx[0, part], 0.0), masked[part], jnp.where(keep_north, rx[1, part], 0.0), zero], axis=0
        )
        high = bands.astype(bf16)
        rest = bands - high.astype(f32)
        mid = rest.astype(bf16)
        low = (rest - mid.astype(f32)).astype(bf16)
        picked = jnp.dot(
            rowcol[...], jnp.concatenate([high, mid, low, jnp.zeros((32, 128), bf16)], axis=0), preferred_element_type=f32
        )
        for b in range(2):
            for rt in range(2):
                acc = zero
                for k in range(4):
                    m = (k * 2 + b) * 16 + rt * 8
                    at = slice(k * 16 + rt * 8, k * 16 + rt * 8 + 8)
                    cell = jnp.take_along_axis(picked[m:m + 8], pt[b, at], axis=1, mode="promise_in_bounds")
                    acc = acc + cell * wt[b, at]
                forcing[b, rt * 64 + f * 8:rt * 64 + f * 8 + 8] = acc

    def forcing_tile(f, rt, b):
        return forcing[b, rt * 64 + f * 8:rt * 64 + f * 8 + 8]

    pack_columns(forcing_tile, 3, fcol_e, fcol_w)

    f_copies = [
        send(fcol_e, rf_w, to_e),
        send(fcol_w, rf_e, to_w),
        send(fcol_e.at[pl.ds(8, 8)], rf_diag.at[3], to_ne),
        send(fcol_w.at[pl.ds(8, 8)], rf_diag.at[2], to_nw),
        send(fcol_e.at[pl.ds(0, 8)], rf_diag.at[1], to_se),
        send(fcol_w.at[pl.ds(0, 8)], rf_diag.at[0], to_sw),
        send(forcing.at[:, pl.ds(64, 24)], rf_ns.at[1], to_n),
        send(forcing.at[:, pl.ds(0, 24)], rf_ns.at[0], to_s),
    ]

    def extended(p, tiles, ns, ce, cw, diag):
        def side(e, w):
            return jnp.where(lane < 64, roll(e, -3 * p, 1), roll(w, 125 - 3 * p, 1))

        rows = []
        for rt in range(2):
            part = slice(rt * 8, rt * 8 + 8)
            rows.append(jnp.concatenate([tiles(p, rt, 0), tiles(p, rt, 1), side(ce[part], cw[part])], axis=1))
        edge = [jnp.where(sub < 4, ns(0, p, b), ns(1, p, b)) for b in range(2)]
        corner = jnp.where(sub < 4, side(diag[0], diag[1]), side(diag[2], diag[3]))
        rows.append(jnp.concatenate(edge + [corner], axis=1))
        return jnp.concatenate(rows, axis=0)

    for c in p_copies:
        c.wait_recv()

    def plane_ns(i, p, b):
        return rns[i, p, :, b * 128:b * 128 + 128]

    height, zonal, meridional, count, top = [
        extended(p, plane_tile, plane_ns, rcol_e, rcol_w, rdiag) for p in range(5)
    ]
    row_ids = subs((24, 384))
    off_grid = ((lat == n_lat - 1) & (row_ids >= 16) & (row_ids < 20)) | ((lat == 0) & (row_ids >= 20))
    count = jnp.where(off_grid, 0.0, count)

    scale = 1.0 / (2.0 * strata)

    def depth(c):
        return c * scale + c * (c - 1.0) * (scale / strata)

    min_e = jnp.minimum(count, east(count))
    min_n = jnp.minimum(count, north(count))
    put(cnt_r, count)
    put(me_r, min_e)
    put(mn_r, min_n)

    def plane_laplace(field):
        fe = jnp.where(whole(me_r) > 0.5, east(field) - field, 0.0)
        fn = jnp.where(whole(mn_r) > 0.5, north(field) - field, 0.0)
        return fe - west(fe) + fn - south(fn)

    wet_own = (own_part(cnt_r) > 0.5).astype(f32)
    top_mix = plane_laplace(plane_laplace(top))[0:16, 0:256]

    def own_forcing(f):
        return jnp.concatenate(
            [jnp.concatenate([forcing_tile(f, rt, 0), forcing_tile(f, rt, 1)], axis=1) for rt in range(2)], axis=0
        )

    heat, light = own_forcing(3), own_forcing(4)
    absorb = 1.0 - math.exp(-1.0 / light_decay)
    t_own = planes[4]
    t_next = jnp.concatenate([tn[0, 16:32], tn[1, 16:32]], axis=1)
    top_part[...] = (
        t_own
        + wet_own
        * (
            diapycnal_diffusion * jnp.where(own_part(cnt_r) > 1.5, t_next - t_own, 0.0)
            + light_gain * absorb * light
            + heat_gain * heat
        )
        - mixing_fourth * top_mix
    )

    for c in t_copies:
        c.wait_recv()

    def unpack(r, _):
        for q in range(8):
            g, q4 = q // 4, q % 4
            at = 2 * r + 32 * q4
            e = pltpu.roll(rt_e[g * 8:g * 8 + 8], lax.rem(256 - at, 128), 1)
            w = pltpu.roll(rt_w[g * 8:g * 8 + 8], lax.rem(254 - at, 128), 1)
            tv[r, q * 8:q * 8 + 8, 256:384] = jnp.where(lane < 64, e, w)
        return 0

    lax.fori_loop(0, 16, unpack, 0, unroll=4)
    for row, r, i in ((16, 0, 0), (23, 15, 2)):
        for q in range(8):
            g, q4 = q // 4, q % 4
            at = 2 * r + 32 * q4
            e = roll(rt_diag[i, g * 8:g * 8 + 8], -at, 1)
            w = roll(rt_diag[i + 1, g * 8:g * 8 + 8], 126 - at, 1)
            tv[row, q * 8:q * 8 + 8, 256:384] = jnp.where(lane < 64, e, w)

    level = subs((8, 384)).astype(f32)

    def wide_row(ref, r):
        return jnp.concatenate([jnp.broadcast_to(ref[b, pl.ds(r, 1), :], (8, 128)) for b in range(3)], axis=1)

    me = wide_row(mn_r, 22)
    for q in range(8):
        part = slice(q * 8, q * 8 + 8)
        flow[part] = jnp.where(level + float(q * 8) < me, tv[23, part] - tv[22, part], 0.0)

    def lap_row(i, _):
        r, rn = lax.rem(i + 23, 24), lax.rem(i, 24)
        me, mn = wide_row(me_r, r), wide_row(mn_r, r)
        for q in range(8):
            part = slice(q * 8, q * 8 + 8)
            lev = level + float(q * 8)
            t = tv[r, part]
            fe = jnp.where(lev < me, east(t) - t, 0.0)
            fn = jnp.where(lev < mn, tv[rn, part] - t, 0.0)
            lap[r, part] = fe - west(fe) + fn - flow[part]
            flow[part] = fn
        return 0

    lax.fori_loop(0, 18, lap_row, 0)

    two = (slice(None), slice(0, 256))
    mn = wide_row(mn_r, 23)[two]
    for q in range(8):
        part = slice(q * 8, q * 8 + 8)
        rise = lap[0, part, 0:256] - lap[23, part, 0:256]
        flow[part, 0:256] = jnp.where(level[two] + float(q * 8) < mn, rise, 0.0)

    def mix_row(r, _):
        me, mn = wide_row(me_r, r), wide_row(mn_r, r)[two]
        for q in range(8):
            part = slice(q * 8, q * 8 + 8)
            lev = level + float(q * 8)
            t = lap[r, part]
            fe = jnp.where(lev < me, east(t) - t, 0.0)
            fn = jnp.where(lev[two] < mn, lap[r + 1, part, 0:256] - t[two], 0.0)
            mix[r, part] = (-mixing_fourth) * ((fe - west(fe))[two] + fn - flow[part, 0:256])
            flow[part, 0:256] = fn
        return 0

    lax.fori_loop(0, 16, mix_row, 0)

    for c in f_copies:
        c.wait_recv()

    def forcing_ns(i, f, b):
        return rf_ns[i, b, f * 8:f * 8 + 8]

    wind_e, wind_n, fresh = [
        extended(f, forcing_tile, forcing_ns, rf_e, rf_w, rf_diag) for f in range(3)
    ]
    min_e, min_n = whole(me_r), whole(mn_r)
    depth_e, depth_n = depth(min_e), depth(min_n)
    pull_e, pull_n = grav_step * depth_e, grav_step * depth_n
    push_e = jnp.where(min_e > 0.5, wind_step * wind_e, 0.0)
    push_n = jnp.where(min_n > 0.5, wind_step * wind_n, 0.0)
    gain = jnp.where(whole(cnt_r) > 0.5, fresh_step * fresh, 0.0)
    zonal = jnp.where(min_e > 0.5, zonal, 0.0)
    meridional = jnp.where(min_n > 0.5, meridional, 0.0)
    for _ in range(SUBS):
        zonal = zonal - pull_e * (east(height) - height) + push_e
        meridional = meridional - pull_n * (north(height) - height) + push_n
        height = height + gain - height_step * (zonal - west(zonal) + meridional - south(meridional))

    own = (slice(0, 16), slice(0, 256))
    o_height[...] = height[own]
    o_zonal[...] = zonal[own]
    o_meridional[...] = meridional[own]
    speed_e = zonal * ((-0.5 * advect_coef) / jnp.maximum(depth_e, depth_floor))
    speed_n = meridional * ((-0.5 * advect_coef) / jnp.maximum(depth_n, depth_floor))
    put(se_r, speed_e)
    put(sn_r, speed_n)

    ce = speed_e * (top + east(top))
    cn = speed_n * (top + north(top))
    top_new = top_part[...] + (ce - west(ce) + cn - south(cn))[own]
    inverse = wet_own / jnp.maximum(depth(own_part(cnt_r)), depth_floor)
    surface = [top_new * wet_own, height[own] * wet_own, zonal[own] * inverse, meridional[own] * inverse, wet_own]
    for s in range(8):
        for b in range(2):
            piece = surface[s][:, b * 128:b * 128 + 128] if s < 5 else jnp.zeros((16, 128), f32)
            sv[pl.ds(b * 8 + s, 16, stride=16), :] = piece

    cell_id = lax.broadcasted_iota(jnp.int32, (128, 128), 0).astype(f32).astype(bf16)

    def spread(r, _):
        for b in range(2):
            value = sv[pl.ds(pl.multiple_of(r * 16 + b * 8, 8), 8), :]
            for k in range(4):
                share = value * wt[b, pl.ds(k * 16 + r, 1), :]
                high = share.astype(bf16)
                low = (share - high.astype(f32)).astype(bf16)
                point = pt[b, pl.ds(k * 16 + r, 1), :].astype(f32).astype(bf16)
                by_cell = lax.dot_general(
                    jnp.concatenate([high, low], axis=0), jnp.where(cell_id == point, bf16(1), bf16(0)),
                    (((1,), (1,)), ((), ())), preferred_element_type=f32,
                )
                cells[pl.ds((k * 2 + b) * 16 + r, 8, stride=128), :] = by_cell[0:8] + by_cell[8:16]
        return 0

    lax.fori_loop(0, 16, spread, 0, unroll=2)

    for s in range(5):
        part = cells[s * 128:s * 128 + 128]
        high = part.astype(bf16)
        low = (part - high.astype(f32)).astype(bf16)
        rows = jnp.dot(row_hot[...], high, preferred_element_type=f32) + jnp.dot(
            row_hot[...], low, preferred_element_type=f32
        )
        for band in range(3):
            table[band, s * 8:s * 8 + 8] = rows[band * 8:band * 8 + 8]

    s_s = send(table.at[0], rtable.at[1], to_s)
    s_n = send(table.at[2], rtable.at[0], to_n)

    def vertical(i, carry):
        fade, below = carry
        below = list(below)
        for j in range(4):
            l = i * 4 + j
            lev = (l + 0).astype(f32)
            for rt in range(2):
                rows = slice(rt * 8, rt * 8 + 8)
                for b in range(2):
                    c = cnt_r[b, rows]
                    at = pl.multiple_of(l * 16 + rt * 8, 8)
                    t = tn[b, pl.ds(at, 8)]
                    up = tn[b, pl.ds(pl.multiple_of(lax.rem(at + 16, 1024), 8), 8)]
                    down = jnp.where(lev + 1.0 < c, up - t, 0.0)
                    source = (fade * (light_gain * absorb * math.exp(-j / light_decay))) * forcing[
                        b, rt * 64 + 32:rt * 64 + 40
                    ]
                    gain = diapycnal_diffusion * (down - below[rt * 2 + b]) + source
                    tpart[b, pl.ds(at, 8)] = t + jnp.where(lev < c, gain, 0.0)
                    below[rt * 2 + b] = down
        return fade * math.exp(-4.0 / light_decay), tuple(below)

    lax.fori_loop(0, strata // 4, vertical, (f32(1.0), (jnp.zeros((8, 128), f32),) * 4))
    for rt in range(2):
        rows = slice(rt * 8, rt * 8 + 8)
        for b in range(2):
            tpart[b, rows] = tpart[b, rows] + jnp.where(
                cnt_r[b, rows] > 0.5, heat_gain * forcing[b, rt * 64 + 24:rt * 64 + 32], 0.0
            )

    mn, vn = wide_row(mn_r, 23)[two], wide_row(sn_r, 23)[two]
    for q in range(8):
        part = slice(q * 8, q * 8 + 8)
        both = tv[0, part, 0:256] + tv[23, part, 0:256]
        flow[part, 0:256] = jnp.where(level[two] + float(q * 8) < mn, vn * both, 0.0)

    def advect_row(r, _):
        me, mn = wide_row(me_r, r), wide_row(mn_r, r)[two]
        ve, vn = wide_row(se_r, r), wide_row(sn_r, r)[two]
        for q in range(8):
            part = slice(q * 8, q * 8 + 8)
            lev = level + float(q * 8)
            t = tv[r, part]
            fe = jnp.where(lev < me, ve * (t + east(t)), 0.0)
            fn = jnp.where(lev[two] < mn, vn * (t[two] + tv[r + 1, part, 0:256]), 0.0)
            change = mix[r, part] + (fe - west(fe))[two] + fn - flow[part, 0:256]
            flow[part, 0:256] = fn
            for b in range(2):
                at = pl.ds(q * 128 + r, 8, stride=16)
                tnew[b, at, :] = tpart[b, at, :] + change[:, b * 128:b * 128 + 128]
        return 0

    lax.fori_loop(0, 16, advect_row, 0)

    s_s.wait_recv()
    s_n.wait_recv()

    def from_bands(s):
        part = slice(s * 8, s * 8 + 8)
        from_south = jnp.where(keep_south, rtable[0, part], 0.0)
        from_north = jnp.where(keep_north, rtable[1, part], 0.0)
        return table[1, part] + from_south + from_north

    factor = (1 - flags[...]).astype(f32) / jnp.maximum(from_bands(4), area_floor)
    for s in range(4):
        o_skin[s * 8:s * 8 + 8] = from_bands(s) * factor
    for c in sends:
        c.wait_send()


def deliver(height, zonal, meridional, thermal, skin, h_out, u_out, v_out, t_out, skin_out, sem):
    rows = t_out.shape[0]
    copies = [(height, h_out), (zonal, u_out), (meridional, v_out), (skin, skin_out)]
    copies += [(thermal.at[b, pl.ds(0, rows)], t_out.at[:, pl.ds(b * 128, 128)]) for b in range(2)]
    copies = [pltpu.make_async_copy(a, b, sem.at[i]) for i, (a, b) in enumerate(copies)]
    for c in copies:
        c.start()
    for c in copies:
        c.wait()


def shards(
    free_elevation, zonal_volume_carriage, meridional_volume_carriage, thermal_field, flooded_strata_number,
    aerial_exchanges, aerial_terrain_flags, donor_tile_number, donor_point_number, pairing_coefficients,
):
    strata = thermal_field.shape[0]
    vmem = pltpu.VMEM
    anywhere = pl.BlockSpec(memory_space=pl.ANY)
    far = pl.BlockSpec(memory_space=pltpu.HBM)
    local = pl.BlockSpec(memory_space=pltpu.VMEM)
    results = pl.pallas_call(
        kernel,
        out_shape=(vmem((16, 256), f32),) * 3 + (vmem((2, 1024, 128), f32), vmem((32, 128), f32)),
        in_specs=[far] * 10,
        out_specs=(local,) * 5,
        scratch_shapes=[
            vmem((5, 16, 256), f32), vmem((16, 256), jnp.int32), vmem((2, 1024, 128), f32), vmem((40, 128), f32),
            vmem((8, 128), jnp.int32), vmem((2, 64, 128), jnp.int32), vmem((2, 64, 128), f32),
            vmem((4, 2, 16), jnp.int32), vmem((8, 128), f32), vmem((40, 128), f32), vmem((2, 40, 128), f32),
            vmem((16, 128), f32), vmem((16, 128), f32), vmem((16, 128), f32), vmem((16, 128), f32),
            vmem((4, 8, 128), f32), vmem((2, 5, 8, 256), f32),
            vmem((24, 64, 384), f32), vmem((2, 16, 128), f32), vmem((16, 128), f32), vmem((16, 128), f32),
            vmem((4, 16, 128), f32),
            vmem((2, 128, 128), f32), vmem((16, 128), f32), vmem((16, 128), f32), vmem((16, 128), f32),
            vmem((16, 128), f32), vmem((4, 8, 128), f32), vmem((2, 2, 24, 128), f32),
            vmem((3, 24, 128), f32), vmem((3, 24, 128), f32), vmem((3, 24, 128), f32), vmem((3, 24, 128), f32),
            vmem((3, 24, 128), f32),
            vmem((24, 64, 384), f32), vmem((16, 64, 256), f32), vmem((2, 1024, 128), f32), vmem((64, 384), f32),
            vmem((128, 128), bf16), vmem((32, 128), bf16), vmem((256, 128), f32), vmem((1024, 128), f32),
            vmem((3, 40, 128), f32), vmem((2, 40, 128), f32), vmem((16, 256), f32),
            pltpu.SemaphoreType.DMA((14,)),
            pltpu.SemaphoreType.DMA((28,)), pltpu.SemaphoreType.DMA((28,)),
        ],
        compiler_params=pltpu.CompilerParams(collective_id=0, has_side_effects=True, vmem_limit_bytes=65929216),
    )(
        free_elevation, zonal_volume_carriage, meridional_volume_carriage, thermal_field.reshape(strata * 16, 256),
        flooded_strata_number, aerial_exchanges.reshape(40, 128), aerial_terrain_flags, donor_tile_number.swapaxes(1, 2),
        donor_point_number.reshape(64, 256), pairing_coefficients.reshape(64, 256),
    )
    plane = jax.ShapeDtypeStruct((16, 256), f32)
    h, u, v, t, skin = pl.pallas_call(
        deliver,
        out_shape=(plane,) * 3 + (jax.ShapeDtypeStruct((strata * 16, 256), f32), jax.ShapeDtypeStruct((32, 128), f32)),
        in_specs=[local] * 5,
        out_specs=(anywhere,) * 5,
        scratch_shapes=[pltpu.SemaphoreType.DMA((6,))],
        compiler_params=pltpu.CompilerParams(vmem_limit_bytes=8 << 20),
    )(*results)
    return h, u, v, t.reshape(strata, 16, 256), skin.reshape(4, 8, 128)


def solution(mesh):
    flat, deep = P("lat", "lon"), P(None, "lat", "lon")
    return jax.shard_map(
        shards,
        mesh=mesh,
        in_specs=(flat, flat, flat, deep, flat, deep, flat, deep, deep, deep),
        out_specs=(flat, flat, flat, deep, deep),
        check_vma=False,
    )
```

```python
import math

import jax
import jax.numpy as jnp
from jax import lax
from jax.experimental import pallas as pl
from jax.experimental.pallas import tpu as pltpu
from jax.sharding import PartitionSpec as P

SUBS = 3
grav_step = 0.6
height_step = 0.6
wind_step = 0.5
fresh_step = 0.5
mixing_fourth = 0.02
advect_coef = 0.1
diapycnal_diffusion = 0.2
heat_gain = 0.3
light_gain = 0.3
light_decay = 8.0
depth_floor = 0.25
area_floor = 1.0
absorb_of = 1.0 - math.exp(-1.0 / light_decay)

f32 = jnp.float32
bf16 = jnp.bfloat16

FLUX_ORDER = (0, 1, 4, 2, 3)


def lanes(shape):
    return lax.broadcasted_iota(jnp.int32, shape, len(shape) - 1)


def subs(shape):
    return lax.broadcasted_iota(jnp.int32, shape, len(shape) - 2)


def roll(x, shift, axis):
    return pltpu.roll(x, shift % x.shape[axis], axis)


def east(x):
    return roll(x, -1, 1)


def west(x):
    return roll(x, 1, 1)


def north(x):
    return roll(x, -1, 0)


def south(x):
    return roll(x, 1, 0)


def put(ref, value):
    for b in range(3):
        ref[b] = value[:, b * 128:b * 128 + 128]


def whole(ref):
    return jnp.concatenate([ref[b] for b in range(3)], axis=1)


def own_part(ref):
    return jnp.concatenate([ref[b, 0:16] for b in range(2)], axis=1)


def kernel(
    h_in, u_in, v_in, t_in, n_in, x_in, flag_in, tile, pt_in, w_in,
    o_height, o_zonal, o_meridional, tnew, o_skin,
    planes, count_int, tn, flux, flags, pt, wt,
    rows_in, rows_wide, masked, rx, col_e, col_w, rcol_e, rcol_w, rdiag, rns,
    tv, tpack, rt_e, rt_w, rt_diag, rt_ns, edge_mix, edge_sum,
    forcing, fcol_e, fcol_w, rf_e, rf_w, rf_diag, rf_ns,
    cnt_r, me_r, mn_r, se_r, sn_r, mc_r, light_r,
    lap, mix, tpart, flow, flow2, rowcol, row_hot, sv, cells, table, rtable, top_part,
    in_sem, send_sem, recv_sem,
):
    strata = t_in.shape[0] // 16
    n_lon, n_lat = lax.axis_size("lon"), lax.axis_size("lat")
    lon, lat = lax.axis_index("lon"), lax.axis_index("lat")
    le, lw = lax.rem(lon + 1, n_lon), lax.rem(lon + n_lon - 1, n_lon)
    ln, ls = lax.rem(lat + 1, n_lat), lax.rem(lat + n_lat - 1, n_lat)
    to_n, to_s = {"lon": lon, "lat": ln}, {"lon": lon, "lat": ls}
    to_e, to_w = {"lon": le, "lat": lat}, {"lon": lw, "lat": lat}
    to_ne, to_nw = {"lon": le, "lat": ln}, {"lon": lw, "lat": ln}
    to_se, to_sw = {"lon": le, "lat": ls}, {"lon": lw, "lat": ls}

    barrier = pltpu.get_barrier_semaphore()
    for where in (to_n, to_s, to_e, to_w, to_ne, to_nw, to_se, to_sw):
        pl.semaphore_signal(barrier, inc=1, device_id=where, device_id_type=pl.DeviceIdType.MESH)

    loads = [
        (x_in, flux), (flag_in, flags), (n_in, count_int), (h_in, planes.at[0]), (u_in, planes.at[1]),
        (v_in, planes.at[2]), (t_in.at[pl.ds(0, 16)], planes.at[4]),
        (pt_in.at[:, pl.ds(0, 128)], pt.at[0]), (pt_in.at[:, pl.ds(128, 128)], pt.at[1]),
        (w_in.at[:, pl.ds(0, 128)], wt.at[0]), (w_in.at[:, pl.ds(128, 128)], wt.at[1]),
        (tile, rows_in), (t_in.at[:, pl.ds(0, 128)], tn.at[0, pl.ds(0, strata * 16)]),
        (t_in.at[:, pl.ds(128, 128)], tn.at[1, pl.ds(0, strata * 16)]),
    ]
    load = [pltpu.make_async_copy(a, b, in_sem.at[i]) for i, (a, b) in enumerate(loads)]
    for c in load:
        c.start()

    sends = []

    def send(src, dst, where):
        i = len(sends)
        c = pltpu.make_async_remote_copy(
            src_ref=src, dst_ref=dst, send_sem=send_sem.at[i], recv_sem=recv_sem.at[i],
            device_id=where, device_id_type=pl.DeviceIdType.MESH,
        )
        c.start()
        sends.append(c)
        return c

    lane = lanes((8, 128))
    sub = subs((8, 128))

    load[0].wait()
    load[1].wait()
    open_sea = (1 - flags[...]).astype(f32)
    for f, g in enumerate(FLUX_ORDER):
        masked[f * 8:f * 8 + 8] = flux[g * 8:g * 8 + 8] * open_sea
    for i in range(2, 7):
        load[i].wait()
    planes[3] = count_int[...].astype(f32)

    def pack_columns(tiles, n, dst_e, dst_w):
        for rt in range(2):
            pe = pw = jnp.zeros((8, 128), f32)
            for p in range(n):
                here = (lane >= 3 * p) & (lane < 3 * p + 3)
                pe = jnp.where(here, roll(tiles(p, rt, 1), 3 * p - 125, 1), pe)
                pw = jnp.where(here, roll(tiles(p, rt, 0), 3 * p, 1), pw)
            dst_e[rt * 8:rt * 8 + 8] = pe
            dst_w[rt * 8:rt * 8 + 8] = pw

    def plane_tile(p, rt, b):
        return planes[p, rt * 8:rt * 8 + 8, b * 128:b * 128 + 128]

    pack_columns(plane_tile, 5, col_e, col_w)

    half = lax.shift_right_logical(lane, 1)

    def do_turn():
        load[12].wait()
        load[13].wait()
        for b in range(2):
            tn[b, strata * 16:] = jnp.zeros((64 * 16 - strata * 16, 128), f32)

        def turn(r, carry):
            carry = list(carry)
            for q in range(8):
                g, q4 = q // 4, q % 4
                here = half == r + 16 * q4
                t0 = tn[0, pl.ds(q * 128 + r, 8, stride=16), :]
                t1 = tn[1, pl.ds(q * 128 + r, 8, stride=16), :]
                tv[r, q * 8:q * 8 + 8, 0:128] = t0
                tv[r, q * 8:q * 8 + 8, 128:256] = t1
                at = 2 * r + 32 * q4
                carry[g] = jnp.where(here, pltpu.roll(t1, lax.rem(at + 2, 128), 1), carry[g])
                carry[2 + g] = jnp.where(here, pltpu.roll(t0, at, 1), carry[2 + g])
            return tuple(carry)

        packs = lax.fori_loop(0, 16, turn, (jnp.zeros((8, 128), f32),) * 4, unroll=4)
        for i in range(4):
            tpack[i // 2, (i % 2) * 8:(i % 2) * 8 + 8] = packs[i]
        for i in range(2):
            packed = jnp.zeros((8, 128), f32)
            for r in range(16):
                row = jnp.broadcast_to(planes[3, r:r + 1, (1 - i) * 128:(1 - i) * 128 + 128], (8, 128))
                packed = jnp.where(half == r, roll(row, 2 * r + 2 * (1 - i), 1), packed)
            tpack[i, 16:24] = spread_groups(packed)

    def spread_groups(x):
        x = jnp.where(lane < 32, x, 0.0)
        x = x + roll(x, 32, 1)
        return x + roll(x, 64, 1)

    two = (slice(None), slice(0, 256))
    level = subs((8, 256)).astype(f32)

    def own_row(ref, r):
        return jnp.concatenate([jnp.broadcast_to(ref[b, pl.ds(r, 1), :], (8, 128)) for b in range(2)], axis=1)

    def start_flow(dst, src, r, rn):
        mn = own_row(mn_r, r)
        for q in range(8):
            part = slice(q * 8, q * 8 + 8)
            dst[part] = jnp.where(level + float(q * 8) < mn, src[rn, part] - src[r, part], 0.0)

    def lap_row(r, _):
        rn = lax.rem(r + 1, 24)
        me, mn = own_row(mc_r, r), own_row(mn_r, r)
        for q in range(8):
            part = slice(q * 8, q * 8 + 8)
            lev = level + float(q * 8)
            t = tv[r, part]
            fe = jnp.where(lev < me, east(t) - t, 0.0)
            fn = jnp.where(lev < mn, tv[rn, part] - t, 0.0)
            lap[r, part] = fe - west(fe) + fn - flow[part]
            flow[part] = fn
        return 0

    def mix_row(r, _):
        me, mn = own_row(mc_r, r), own_row(mn_r, r)
        for q in range(8):
            part = slice(q * 8, q * 8 + 8)
            lev = level + float(q * 8)
            t = lap[r, part]
            fe = jnp.where(lev < me, east(t) - t, 0.0)
            fn = jnp.where(lev < mn, lap[r + 1, part] - t, 0.0)
            mix[r, part] = (-mixing_fourth) * (fe - west(fe) + fn - flow2[part])
            flow2[part] = fn
        return 0

    def do_inner():
        start_flow(flow, tv, 0, 1)
        lax.fori_loop(1, 15, lap_row, 0)
        start_flow(flow2, lap, 1, 2)
        lax.fori_loop(2, 14, mix_row, 0)

    def do_vertical():
        def vertical(i, below):
            below = list(below)
            for j in range(4):
                l = i * 4 + j
                lev = l.astype(f32)
                for rt in range(2):
                    for b in range(2):
                        c = planes[3, rt * 8:rt * 8 + 8, b * 128:b * 128 + 128]
                        at = pl.multiple_of(l * 16 + rt * 8, 8)
                        t = tn[b, pl.ds(at, 8)]
                        up = tn[b, pl.ds(pl.multiple_of(lax.rem(at + 16, 1024), 8), 8)]
                        down = jnp.where(lev + 1.0 < c, up - t, 0.0)
                        gain = diapycnal_diffusion * (down - below[rt * 2 + b])
                        tpart[b, pl.ds(at, 8)] = t + jnp.where(lev < c, gain, 0.0)
                        below[rt * 2 + b] = down
            return tuple(below)

        lax.fori_loop(0, strata // 4, vertical, (jnp.zeros((8, 128), f32),) * 4)

    c_own = planes[3]
    c_east = jnp.where(lanes((16, 256)) == 255, 0.0, jnp.minimum(c_own, east(c_own)))
    c_north = jnp.minimum(c_own, north(c_own))
    for b in range(2):
        mc_r[b, 0:16] = c_east[:, b * 128:b * 128 + 128]
        mn_r[b, 0:16] = c_north[:, b * 128:b * 128 + 128]

    early = lax.rem(lon, n_lon // 2) < n_lon // 4

    @pl.when(early)
    def _():
        do_turn()
        do_vertical()
        do_inner()

    pl.semaphore_wait(barrier, 8)

    x_n = send(masked, rx.at[0], to_n)
    x_s = send(masked, rx.at[1], to_s)
    p_copies = [
        send(col_e, rcol_w, to_e),
        send(col_w, rcol_e, to_w),
        send(col_e.at[pl.ds(8, 8)], rdiag.at[3], to_ne),
        send(col_w.at[pl.ds(8, 8)], rdiag.at[2], to_nw),
        send(col_e.at[pl.ds(0, 8)], rdiag.at[1], to_se),
        send(col_w.at[pl.ds(0, 8)], rdiag.at[0], to_sw),
        send(planes.at[:, pl.ds(8, 8)], rns.at[1], to_n),
        send(planes.at[:, pl.ds(0, 8)], rns.at[0], to_s),
    ]

    load[11].wait()
    for j in range(8):
        rows_wide[j:j + 1, 0:16] = rows_in[j // 2, j % 2:j % 2 + 1, :].astype(f32)
    row_of = jnp.zeros((8, 128), f32)
    for j in range(8):
        here = lax.shift_right_logical(lane, 4) == j
        row_of = jnp.where(here, roll(jnp.broadcast_to(rows_wide[j:j + 1, :], (8, 128)), 16 * j, 1), row_of)
    row_id = subs((128, 128))
    hot = (row_id & 31).astype(f32) == jnp.concatenate([row_of] * 16, axis=0)
    hot = jnp.where(hot & (row_id < 96), 1.0, 0.0)
    row_hot[...] = hot[0:32].astype(bf16)
    rowcol[...] = jnp.transpose(hot).astype(bf16)

    @pl.when(jnp.logical_not(early))
    def _():
        do_turn()

    t_copies = [
        send(tpack.at[0], rt_w, to_e),
        send(tpack.at[1], rt_e, to_w),
        send(tpack.at[0], rt_diag.at[3], to_ne),
        send(tpack.at[1], rt_diag.at[2], to_nw),
        send(tpack.at[0], rt_diag.at[1], to_se),
        send(tpack.at[1], rt_diag.at[0], to_sw),
        send(tv.at[pl.ds(14, 2)], tv.at[pl.ds(22, 2)], to_n),
        send(tv.at[pl.ds(0, 2)], tv.at[pl.ds(16, 2)], to_s),
        send(tpack, rt_ns.at[1], to_n),
        send(tpack, rt_ns.at[0], to_s),
    ]

    for i in range(7, 11):
        load[i].wait()

    @pl.when(jnp.logical_not(early))
    def _():
        do_vertical()

    x_n.wait_recv()
    x_s.wait_recv()
    keep_south = jnp.broadcast_to(lat, (8, 128)) > 0
    keep_north = jnp.broadcast_to(lat, (8, 128)) < n_lat - 1
    zero = jnp.zeros((8, 128), f32)
    for f in range(5):
        part = slice(f * 8, f * 8 + 8)
        bands = jnp.concatenate(
            [jnp.where(keep_south, rx[0, part], 0.0), masked[part], jnp.where(keep_north, rx[1, part], 0.0), zero], axis=0
        )
        high = bands.astype(bf16)
        rest = bands - high.astype(f32)
        mid = rest.astype(bf16)
        low = (rest - mid.astype(f32)).astype(bf16)
        picked = jnp.dot(
            rowcol[...], jnp.concatenate([high, mid, low, jnp.zeros((32, 128), bf16)], axis=0), preferred_element_type=f32
        )
        for b in range(2):
            for rt in range(2):
                acc = zero
                for k in range(4):
                    m = (k * 2 + b) * 16 + rt * 8
                    at = slice(k * 16 + rt * 8, k * 16 + rt * 8 + 8)
                    cell = jnp.take_along_axis(picked[m:m + 8], pt[b, at], axis=1, mode="promise_in_bounds")
                    acc = acc + cell * wt[b, at]
                forcing[b, rt * 64 + f * 8:rt * 64 + f * 8 + 8] = acc

    def forcing_tile(f, rt, b):
        return forcing[b, rt * 64 + f * 8:rt * 64 + f * 8 + 8]

    pack_columns(forcing_tile, 3, fcol_e, fcol_w)

    f_copies = [
        send(fcol_e, rf_w, to_e),
        send(fcol_w, rf_e, to_w),
        send(fcol_e.at[pl.ds(8, 8)], rf_diag.at[3], to_ne),
        send(fcol_w.at[pl.ds(8, 8)], rf_diag.at[2], to_nw),
        send(fcol_e.at[pl.ds(0, 8)], rf_diag.at[1], to_se),
        send(fcol_w.at[pl.ds(0, 8)], rf_diag.at[0], to_sw),
        send(forcing.at[:, pl.ds(64, 24)], rf_ns.at[1], to_n),
        send(forcing.at[:, pl.ds(0, 24)], rf_ns.at[0], to_s),
    ]

    def extended(p, tiles, ns, ce, cw, diag):
        def side(e, w):
            return jnp.where(lane < 64, roll(e, -3 * p, 1), roll(w, 125 - 3 * p, 1))

        rows = []
        for rt in range(2):
            part = slice(rt * 8, rt * 8 + 8)
            rows.append(jnp.concatenate([tiles(p, rt, 0), tiles(p, rt, 1), side(ce[part], cw[part])], axis=1))
        edge = [jnp.where(sub < 4, ns(0, p, b), ns(1, p, b)) for b in range(2)]
        corner = jnp.where(sub < 4, side(diag[0], diag[1]), side(diag[2], diag[3]))
        rows.append(jnp.concatenate(edge + [corner], axis=1))
        return jnp.concatenate(rows, axis=0)

    for c in p_copies:
        c.wait_recv()

    def plane_ns(i, p, b):
        return rns[i, p, :, b * 128:b * 128 + 128]

    height, zonal, meridional, count, top = [
        extended(p, plane_tile, plane_ns, rcol_e, rcol_w, rdiag) for p in range(5)
    ]
    row_ids = subs((24, 384))
    off_grid = ((lat == n_lat - 1) & (row_ids >= 16) & (row_ids < 20)) | ((lat == 0) & (row_ids >= 20))
    count = jnp.where(off_grid, 0.0, count)

    scale = 1.0 / (2.0 * strata)

    def depth(c):
        return c * scale + c * (c - 1.0) * (scale / strata)

    min_e = jnp.minimum(count, east(count))
    min_n = jnp.minimum(count, north(count))
    put(cnt_r, count)
    put(me_r, min_e)
    put(mn_r, min_n)
    closed = jnp.where(lanes((24, 384)) == 255, 0.0, min_e)
    for b in range(2):
        mc_r[b] = closed[:, b * 128:b * 128 + 128]

    def plane_laplace(field):
        fe = jnp.where(whole(me_r) > 0.5, east(field) - field, 0.0)
        fn = jnp.where(whole(mn_r) > 0.5, north(field) - field, 0.0)
        return fe - west(fe) + fn - south(fn)

    wet_own = (own_part(cnt_r) > 0.5).astype(f32)
    top_mix = plane_laplace(plane_laplace(top))[0:16, 0:256]

    def own_forcing(f):
        return jnp.concatenate(
            [jnp.concatenate([forcing_tile(f, rt, 0), forcing_tile(f, rt, 1)], axis=1) for rt in range(2)], axis=0
        )

    heat, light = own_forcing(3), own_forcing(4)
    for b in range(2):
        light_r[b] = (light_gain * absorb_of) * light[:, b * 128:b * 128 + 128]
    t_own = planes[4]
    t_next = jnp.concatenate([tn[0, 16:32], tn[1, 16:32]], axis=1)
    top_part[...] = (
        t_own
        + wet_own
        * (
            diapycnal_diffusion * jnp.where(own_part(cnt_r) > 1.5, t_next - t_own, 0.0)
            + light_gain * absorb_of * light
            + heat_gain * heat
        )
        - mixing_fourth * top_mix
    )

    for c in t_copies:
        c.wait_recv()

    @pl.when(jnp.logical_not(early))
    def _():
        do_inner()

    lax.fori_loop(15, 17, lap_row, 0)
    start_flow(flow, tv, 22, 23)
    lax.fori_loop(0, 2, lambda i, _: lap_row(lax.rem(i + 23, 24), 0), 0)
    lax.fori_loop(14, 16, mix_row, 0)
    start_flow(flow2, lap, 23, 0)
    lax.fori_loop(0, 2, mix_row, 0)

    odd = (lane & 1) == 1
    group_lane = lane & 31
    keep_s, keep_n = keep_south, keep_north

    def edge(side):
        beside = rt_e if side == 0 else rt_w
        diag_n, diag_s = (rt_diag.at[0], rt_diag.at[2]) if side == 0 else (rt_diag.at[1], rt_diag.at[3])

        def join(own_pack, other):
            return jnp.where(odd, own_pack, other) if side == 0 else jnp.where(odd, other, own_pack)

        def shift_out(own_pack, other):
            return jnp.where(odd, roll(other, 1, 1), roll(other, -1, 1)) if side == 0 else jnp.where(
                odd, roll(other, 1, 1), roll(other, -1, 1)
            )

        def shift_in(own_pack, other):
            return jnp.where(odd, roll(own_pack, 1, 1), roll(own_pack, -1, 1))

        def up(x, x_n):
            return jnp.where(group_lane >= 30, roll(x_n, 30, 1), roll(x, -2, 1))

        def down(x, x_s):
            return jnp.where(group_lane < 2, roll(x_s, -30, 1), roll(x, 2, 1))

        mine = jnp.logical_not(odd) if side == 1 else odd
        back = 1 if side == 0 else -1
        rows = slice(16, 24)
        c = join(tpack[side, rows], beside[rows])
        c_out, c_in = shift_out(tpack[side, rows], beside[rows]), shift_in(tpack[side, rows], beside[rows])
        cn_pack = jnp.where(keep_n, join(rt_ns[0, side, rows], diag_n[rows]), 0.0)
        cs_pack = jnp.where(keep_s, join(rt_ns[1, side, rows], diag_s[rows]), 0.0)
        cn_out = jnp.where(keep_n, shift_out(rt_ns[0, side, rows], diag_n[rows]), 0.0)
        cs_out = jnp.where(keep_s, shift_out(rt_ns[1, side, rows], diag_s[rows]), 0.0)
        m_out, m_in = jnp.minimum(c, c_out), jnp.minimum(c, c_in)
        m_n, m_s = jnp.minimum(c, up(c, cn_pack)), jnp.minimum(c, down(c, cs_pack))
        m_n_out, m_s_out = jnp.minimum(cn_pack, cn_out), jnp.minimum(cs_pack, cs_out)
        for g in range(2):
            part = slice(g * 8, g * 8 + 8)
            lev = (sub + 8 * (4 * g + lax.shift_right_logical(lane, 5))).astype(f32)
            own_pack, other = tpack[side, part], beside[part]
            own_n, other_n = rt_ns[0, side, part], diag_n[part]
            own_s, other_s = rt_ns[1, side, part], diag_s[part]
            z = join(own_pack, other)
            z_n, z_s = join(own_n, other_n), join(own_s, other_s)
            z_out = shift_out(own_pack, other)
            flux_out = jnp.where(lev < m_out, z_out - z, 0.0)
            flux_in = jnp.where(lev < m_in, shift_in(own_pack, other) - z, 0.0)
            flux_n = jnp.where(lev < m_n, up(z, z_n) - z, 0.0)
            flux_s = jnp.where(lev < m_s, down(z, z_s) - z, 0.0)
            full = flux_out + flux_in + flux_n + flux_s
            missing = jnp.where(mine, flux_out, 0.0)
            missing_n = jnp.where(lev < m_n_out, shift_out(own_n, other_n) - z_n, 0.0)
            missing_s = jnp.where(lev < m_s_out, shift_out(own_s, other_s) - z_s, 0.0)
            inward = jnp.where(lev < m_in, missing, 0.0)
            change = (
                jnp.where(lev < m_out, roll(full, back, 1) - full, 0.0)
                - inward
                + jnp.where(lev < m_n, up(missing, missing_n) - missing, 0.0)
                + jnp.where(lev < m_s, down(missing, missing_s) - missing, 0.0)
            )
            change = jnp.where(mine, change, roll(inward, -back, 1))
            edge_mix[side, part] = (-mixing_fourth) * change
            edge_sum[side, part] = jnp.where(mine & (lev < m_out), z_out + z, 0.0)

    edge(0)
    edge(1)

    for c in f_copies:
        c.wait_recv()

    def forcing_ns(i, f, b):
        return rf_ns[i, b, f * 8:f * 8 + 8]

    wind_e, wind_n, fresh = [
        extended(f, forcing_tile, forcing_ns, rf_e, rf_w, rf_diag) for f in range(3)
    ]
    min_e, min_n = whole(me_r), whole(mn_r)
    depth_e, depth_n = depth(min_e), depth(min_n)
    pull_e, pull_n = grav_step * depth_e, grav_step * depth_n
    push_e = jnp.where(min_e > 0.5, wind_step * wind_e, 0.0)
    push_n = jnp.where(min_n > 0.5, wind_step * wind_n, 0.0)
    gain = jnp.where(whole(cnt_r) > 0.5, fresh_step * fresh, 0.0)
    zonal = jnp.where(min_e > 0.5, zonal, 0.0)
    meridional = jnp.where(min_n > 0.5, meridional, 0.0)
    for _ in range(SUBS):
        zonal = zonal - pull_e * (east(height) - height) + push_e
        meridional = meridional - pull_n * (north(height) - height) + push_n
        height = height + gain - height_step * (zonal - west(zonal) + meridional - south(meridional))

    own = (slice(0, 16), slice(0, 256))
    o_height[...] = height[own]
    o_zonal[...] = zonal[own]
    o_meridional[...] = meridional[own]
    speed_e = zonal * ((-0.5 * advect_coef) / jnp.maximum(depth_e, depth_floor))
    speed_n = meridional * ((-0.5 * advect_coef) / jnp.maximum(depth_n, depth_floor))
    put(se_r, speed_e)
    put(sn_r, speed_n)

    ce = speed_e * (top + east(top))
    cn = speed_n * (top + north(top))
    top_new = top_part[...] + (ce - west(ce) + cn - south(cn))[own]
    inverse = wet_own / jnp.maximum(depth(own_part(cnt_r)), depth_floor)
    surface = [top_new * wet_own, height[own] * wet_own, zonal[own] * inverse, meridional[own] * inverse, wet_own]
    for s in range(8):
        for b in range(2):
            piece = surface[s][:, b * 128:b * 128 + 128] if s < 5 else jnp.zeros((16, 128), f32)
            sv[pl.ds(b * 8 + s, 16, stride=16), :] = piece

    cell_id = lax.broadcasted_iota(jnp.int32, (128, 128), 0).astype(f32).astype(bf16)

    wide_id = jnp.concatenate([cell_id, cell_id], axis=1)
    blank = jnp.zeros((16, 128), bf16)

    def spread(r, _):
        value = sv[pl.ds(pl.multiple_of(r * 16, 16), 16), :]
        for k in range(4):
            parts, points = [], []
            for b in range(2):
                share = value[b * 8:b * 8 + 8] * wt[b, pl.ds(k * 16 + r, 1), :]
                high = share.astype(bf16)
                low = (share - high.astype(f32)).astype(bf16)
                parts.append(jnp.concatenate([high, low], axis=0))
                points.append(pt[b, pl.ds(k * 16 + r, 1), :].astype(f32).astype(bf16))
            left = jnp.concatenate(
                [jnp.concatenate([parts[0], blank], axis=1), jnp.concatenate([blank, parts[1]], axis=1)], axis=0
            )
            match = jnp.where(wide_id == jnp.concatenate(points, axis=1), bf16(1), bf16(0))
            by_cell = lax.dot_general(left, match, (((1,), (1,)), ((), ())), preferred_element_type=f32)
            for b in range(2):
                both = by_cell[b * 16:b * 16 + 8] + by_cell[b * 16 + 8:b * 16 + 16]
                cells[pl.ds((k * 2 + b) * 16 + r, 8, stride=128), :] = both
        return 0

    lax.fori_loop(0, 16, spread, 0, unroll=2)

    for s in range(5):
        part = cells[s * 128:s * 128 + 128]
        high = part.astype(bf16)
        low = (part - high.astype(f32)).astype(bf16)
        rows = jnp.dot(row_hot[...], high, preferred_element_type=f32) + jnp.dot(
            row_hot[...], low, preferred_element_type=f32
        )
        for band in range(3):
            table[band, s * 8:s * 8 + 8] = rows[band * 8:band * 8 + 8]

    s_s = send(table.at[0], rtable.at[1], to_s)
    s_n = send(table.at[2], rtable.at[0], to_n)

    for side in range(2):
        lane_of = (lane & 1) == 1 if side == 0 else (lane & 1) == 0
        packed = zero
        for r in range(16):
            row = jnp.broadcast_to(se_r[1 + side, r:r + 1, :], (8, 128))
            here = lane == 2 * r + 1 - side
            packed = jnp.where(here, roll(row, 2 * r + 1 - side - 127, 1), packed)
        speed = spread_groups(packed)
        sign = 1.0 if side == 0 else -1.0
        for g in range(2):
            part = slice(g * 8, g * 8 + 8)
            edge_mix[side, part] = edge_mix[side, part] + sign * speed * edge_sum[side, part]

    mn, vn = own_row(mn_r, 23), own_row(sn_r, 23)
    for q in range(8):
        part = slice(q * 8, q * 8 + 8)
        flow[part] = jnp.where(level + float(q * 8) < mn, vn * (tv[0, part] + tv[23, part]), 0.0)

    fade = jnp.exp(-level / light_decay)

    def advect_row(r, _):
        me, mn = own_row(mc_r, r), own_row(mn_r, r)
        ve, vn = own_row(se_r, r), own_row(sn_r, r)
        cnt, light = own_row(cnt_r, r), own_row(light_r, r) * fade
        for q in range(8):
            part = slice(q * 8, q * 8 + 8)
            lev = level + float(q * 8)
            t = tv[r, part]
            fe = jnp.where(lev < me, ve * (t + east(t)), 0.0)
            fn = jnp.where(lev < mn, vn * (t + tv[r + 1, part]), 0.0)
            source = jnp.where(lev < cnt, light * math.exp(-q * 8 / light_decay), 0.0)
            change = mix[r, part] + (fe - west(fe)) + (fn - flow[part]) + source
            flow[part] = fn
            g, at = q // 4, 2 * r + 32 * (q % 4)
            rows = slice(g * 8, g * 8 + 8)
            edge_w = jnp.where(lane < 2, pltpu.roll(edge_mix[1, rows], lax.rem(128 - at, 128), 1), 0.0)
            edge_e = jnp.where(lane >= 126, pltpu.roll(edge_mix[0, rows], lax.rem(254 - at, 128), 1), 0.0)
            at = pl.ds(q * 128 + r, 8, stride=16)
            tnew[0, at, :] = tpart[0, at, :] + (change[:, 0:128] + edge_w)
            tnew[1, at, :] = tpart[1, at, :] + (change[:, 128:256] + edge_e)
        return 0

    lax.fori_loop(0, 16, advect_row, 0)
    for rt in range(2):
        rows = slice(rt * 8, rt * 8 + 8)
        for b in range(2):
            tnew[b, rows] = tnew[b, rows] + jnp.where(
                cnt_r[b, rows] > 0.5, heat_gain * forcing[b, rt * 64 + 24:rt * 64 + 32], 0.0
            )

    s_s.wait_recv()
    s_n.wait_recv()

    def from_bands(s):
        part = slice(s * 8, s * 8 + 8)
        from_south = jnp.where(keep_south, rtable[0, part], 0.0)
        from_north = jnp.where(keep_north, rtable[1, part], 0.0)
        return table[1, part] + from_south + from_north

    factor = (1 - flags[...]).astype(f32) / jnp.maximum(from_bands(4), area_floor)
    for s in range(4):
        o_skin[s * 8:s * 8 + 8] = from_bands(s) * factor
    for c in sends:
        c.wait_send()


def deliver(height, zonal, meridional, thermal, skin, h_out, u_out, v_out, t_out, skin_out, sem):
    rows = t_out.shape[0]
    copies = [(height, h_out), (zonal, u_out), (meridional, v_out), (skin, skin_out)]
    copies += [(thermal.at[b, pl.ds(0, rows)], t_out.at[:, pl.ds(b * 128, 128)]) for b in range(2)]
    copies = [pltpu.make_async_copy(a, b, sem.at[i]) for i, (a, b) in enumerate(copies)]
    for c in copies:
        c.start()
    for c in copies:
        c.wait()


def shards(
    free_elevation, zonal_volume_carriage, meridional_volume_carriage, thermal_field, flooded_strata_number,
    aerial_exchanges, aerial_terrain_flags, donor_tile_number, donor_point_number, pairing_coefficients,
):
    strata = thermal_field.shape[0]
    vmem = pltpu.VMEM
    anywhere = pl.BlockSpec(memory_space=pl.ANY)
    far = pl.BlockSpec(memory_space=pltpu.HBM)
    local = pl.BlockSpec(memory_space=pltpu.VMEM)
    results = pl.pallas_call(
        kernel,
        out_shape=(vmem((16, 256), f32),) * 3 + (vmem((2, 1024, 128), f32), vmem((32, 128), f32)),
        in_specs=[far] * 10,
        out_specs=(local,) * 5,
        scratch_shapes=[
            vmem((5, 16, 256), f32), vmem((16, 256), jnp.int32), vmem((2, 1024, 128), f32), vmem((40, 128), f32),
            vmem((8, 128), jnp.int32), vmem((2, 64, 128), jnp.int32), vmem((2, 64, 128), f32),
            vmem((4, 2, 16), jnp.int32), vmem((8, 128), f32), vmem((40, 128), f32), vmem((2, 40, 128), f32),
            vmem((16, 128), f32), vmem((16, 128), f32), vmem((16, 128), f32), vmem((16, 128), f32),
            vmem((4, 8, 128), f32), vmem((2, 5, 8, 256), f32),
            vmem((24, 64, 256), f32), vmem((2, 24, 128), f32), vmem((24, 128), f32), vmem((24, 128), f32),
            vmem((4, 24, 128), f32), vmem((2, 2, 24, 128), f32), vmem((2, 16, 128), f32), vmem((2, 16, 128), f32),
            vmem((2, 128, 128), f32), vmem((16, 128), f32), vmem((16, 128), f32), vmem((16, 128), f32),
            vmem((16, 128), f32), vmem((4, 8, 128), f32), vmem((2, 2, 24, 128), f32),
            vmem((3, 24, 128), f32), vmem((3, 24, 128), f32), vmem((3, 24, 128), f32), vmem((3, 24, 128), f32),
            vmem((3, 24, 128), f32), vmem((2, 24, 128), f32), vmem((2, 16, 128), f32),
            vmem((24, 64, 256), f32), vmem((16, 64, 256), f32), vmem((2, 1024, 128), f32), vmem((64, 256), f32), vmem((64, 256), f32),
            vmem((128, 128), bf16), vmem((32, 128), bf16), vmem((256, 128), f32), vmem((1024, 128), f32),
            vmem((3, 40, 128), f32), vmem((2, 40, 128), f32), vmem((16, 256), f32),
            pltpu.SemaphoreType.DMA((14,)),
            pltpu.SemaphoreType.DMA((30,)), pltpu.SemaphoreType.DMA((30,)),
        ],
        compiler_params=pltpu.CompilerParams(collective_id=0, has_side_effects=True, vmem_limit_bytes=65929216),
    )(
        free_elevation, zonal_volume_carriage, meridional_volume_carriage, thermal_field.reshape(strata * 16, 256),
        flooded_strata_number, aerial_exchanges.reshape(40, 128), aerial_terrain_flags, donor_tile_number.swapaxes(1, 2),
        donor_point_number.reshape(64, 256), pairing_coefficients.reshape(64, 256),
    )
    plane = jax.ShapeDtypeStruct((16, 256), f32)
    h, u, v, t, skin = pl.pallas_call(
        deliver,
        out_shape=(plane,) * 3 + (jax.ShapeDtypeStruct((strata * 16, 256), f32), jax.ShapeDtypeStruct((32, 128), f32)),
        in_specs=[local] * 5,
        out_specs=(anywhere,) * 5,
        scratch_shapes=[pltpu.SemaphoreType.DMA((6,))],
        compiler_params=pltpu.CompilerParams(vmem_limit_bytes=8 << 20),
    )(*results)
    return h, u, v, t.reshape(strata, 16, 256), skin.reshape(4, 8, 128)


def solution(mesh):
    flat, deep = P("lat", "lon"), P(None, "lat", "lon")
    return jax.shard_map(
        shards,
        mesh=mesh,
        in_specs=(flat, flat, flat, deep, flat, deep, flat, deep, deep, deep),
        out_specs=(flat, flat, flat, deep, deep),
        check_vma=False,
    )
```

```python
import math

import jax
import jax.numpy as jnp
from jax import lax
from jax.experimental import pallas as pl
from jax.experimental.pallas import tpu as pltpu
from jax.sharding import PartitionSpec as P

SUBS = 3
grav_step = 0.6
height_step = 0.6
wind_step = 0.5
fresh_step = 0.5
mixing_fourth = 0.02
advect_coef = 0.1
diapycnal_diffusion = 0.2
heat_gain = 0.3
light_gain = 0.3
light_decay = 8.0
depth_floor = 0.25
area_floor = 1.0
absorb_of = 1.0 - math.exp(-1.0 / light_decay)

f32 = jnp.float32
bf16 = jnp.bfloat16

FLUX_ORDER = (0, 1, 4, 2, 3)


def lanes(shape):
    return lax.broadcasted_iota(jnp.int32, shape, len(shape) - 1)


def subs(shape):
    return lax.broadcasted_iota(jnp.int32, shape, len(shape) - 2)


def roll(x, shift, axis):
    return pltpu.roll(x, shift % x.shape[axis], axis)


def east(x):
    return roll(x, -1, 1)


def west(x):
    return roll(x, 1, 1)


def north(x):
    return roll(x, -1, 0)


def south(x):
    return roll(x, 1, 0)


def put(ref, value):
    for b in range(3):
        ref[b] = value[:, b * 128:b * 128 + 128]


def whole(ref):
    return jnp.concatenate([ref[b] for b in range(3)], axis=1)


def own_part(ref):
    return jnp.concatenate([ref[b, 0:16] for b in range(2)], axis=1)


def kernel(
    h_in, u_in, v_in, t_in, n_in, x_in, flag_in, tile, pt_in, w_in,
    o_height, o_zonal, o_meridional, tnew, o_skin,
    planes, count_int, tn, flux, flags, pt, wt,
    rows_in, rows_wide, masked, rx, col_e, col_w, rcol_e, rcol_w, rdiag, rns,
    tv, tpack, rt_e, rt_w, rt_diag, rt_ns, edge_mix, edge_sum, edge_all,
    forcing, fcol_e, fcol_w, rf_e, rf_w, rf_diag, rf_ns,
    cnt_r, me_r, mn_r, se_r, sn_r, mc_r, light_r,
    lap, mix, tpart, flow, flow2, face_e, face_n, rowcol, row_hot, sv, cells, table, rtable, top_part,
    in_sem, send_sem, recv_sem,
):
    strata = t_in.shape[0] // 16
    n_lon, n_lat = lax.axis_size("lon"), lax.axis_size("lat")
    lon, lat = lax.axis_index("lon"), lax.axis_index("lat")
    le, lw = lax.rem(lon + 1, n_lon), lax.rem(lon + n_lon - 1, n_lon)
    ln, ls = lax.rem(lat + 1, n_lat), lax.rem(lat + n_lat - 1, n_lat)
    to_n, to_s = {"lon": lon, "lat": ln}, {"lon": lon, "lat": ls}
    to_e, to_w = {"lon": le, "lat": lat}, {"lon": lw, "lat": lat}
    to_ne, to_nw = {"lon": le, "lat": ln}, {"lon": lw, "lat": ln}
    to_se, to_sw = {"lon": le, "lat": ls}, {"lon": lw, "lat": ls}

    barrier = pltpu.get_barrier_semaphore()
    has_n, has_s = lat < n_lat - 1, lat > 0

    def greet(*places):
        for where in places:
            pl.semaphore_signal(barrier, inc=1, device_id=where, device_id_type=pl.DeviceIdType.MESH)

    greet(to_e, to_w)
    pl.when(has_n)(lambda: greet(to_ne, to_nw, to_n))
    pl.when(has_s)(lambda: greet(to_se, to_sw, to_s))

    loads = [
        (x_in, flux), (flag_in, flags), (n_in, count_int), (h_in, planes.at[0]), (u_in, planes.at[1]),
        (v_in, planes.at[2]), (t_in.at[pl.ds(0, 16)], planes.at[4]),
        (pt_in.at[:, pl.ds(0, 128)], pt.at[0]), (pt_in.at[:, pl.ds(128, 128)], pt.at[1]),
        (w_in.at[:, pl.ds(0, 128)], wt.at[0]), (w_in.at[:, pl.ds(128, 128)], wt.at[1]),
        (tile, rows_in), (t_in.at[:, pl.ds(0, 128)], tn.at[0, pl.ds(0, strata * 16)]),
        (t_in.at[:, pl.ds(128, 128)], tn.at[1, pl.ds(0, strata * 16)]),
    ]
    load = [pltpu.make_async_copy(a, b, in_sem.at[i]) for i, (a, b) in enumerate(loads)]
    for c in load:
        c.start()

    sends = []

    groups = {id(to_e): 0, id(to_w): 0, id(to_n): 1, id(to_ne): 1, id(to_nw): 1, id(to_s): 2, id(to_se): 2, id(to_sw): 2}

    def plan(src, dst, where):
        i = len(sends)
        c = pltpu.make_async_remote_copy(
            src_ref=src, dst_ref=dst, send_sem=send_sem.at[i], recv_sem=recv_sem.at[i],
            device_id=where, device_id_type=pl.DeviceIdType.MESH,
        )
        sends.append(c)
        return groups[id(where)], c

    def each(copies, act, north_if, south_if):
        def run(group):
            for g, c in copies:
                if g == group:
                    act(c)

        run(0)
        if any(g == 1 for g, _ in copies):
            pl.when(north_if)(lambda: run(1))
        if any(g == 2 for g, _ in copies):
            pl.when(south_if)(lambda: run(2))

    def start(copies):
        each(copies, lambda c: c.start(), has_n, has_s)

    def arrive(copies):
        each(copies, lambda c: c.wait_recv(), has_s, has_n)

    def leave(copies):
        each(copies, lambda c: c.wait_send(), has_n, has_s)

    lane = lanes((8, 128))
    sub = subs((8, 128))

    load[0].wait()
    load[1].wait()
    open_sea = (1 - flags[...]).astype(f32)
    for f, g in enumerate(FLUX_ORDER):
        masked[f * 8:f * 8 + 8] = flux[g * 8:g * 8 + 8] * open_sea
    for i in range(2, 7):
        load[i].wait()
    planes[3] = count_int[...].astype(f32)

    def pack_columns(tiles, n, dst_e, dst_w):
        for rt in range(2):
            pe = pw = jnp.zeros((8, 128), f32)
            for p in range(n):
                here = (lane >= 3 * p) & (lane < 3 * p + 3)
                pe = jnp.where(here, roll(tiles(p, rt, 1), 3 * p - 125, 1), pe)
                pw = jnp.where(here, roll(tiles(p, rt, 0), 3 * p, 1), pw)
            dst_e[rt * 8:rt * 8 + 8] = pe
            dst_w[rt * 8:rt * 8 + 8] = pw

    def plane_tile(p, rt, b):
        return planes[p, rt * 8:rt * 8 + 8, b * 128:b * 128 + 128]

    pack_columns(plane_tile, 5, col_e, col_w)

    half = lax.shift_right_logical(lane, 1)

    def do_turn():
        load[12].wait()
        load[13].wait()
        for b in range(2):
            tn[b, strata * 16:] = jnp.zeros((64 * 16 - strata * 16, 128), f32)

        def turn(r, carry):
            carry = list(carry)
            for q in range(8):
                g, q4 = q // 4, q % 4
                here = half == r + 16 * q4
                t0 = tn[0, pl.ds(q * 128 + r, 8, stride=16), :]
                t1 = tn[1, pl.ds(q * 128 + r, 8, stride=16), :]
                tv[r, q * 8:q * 8 + 8, 0:128] = t0
                tv[r, q * 8:q * 8 + 8, 128:256] = t1
                at = 2 * r + 32 * q4
                carry[g] = jnp.where(here, pltpu.roll(t1, (at + 2) & 127, 1), carry[g])
                carry[2 + g] = jnp.where(here, pltpu.roll(t0, at, 1), carry[2 + g])
            return tuple(carry)

        packs = lax.fori_loop(0, 16, turn, (jnp.zeros((8, 128), f32),) * 4, unroll=4)
        for i in range(4):
            tpack[i // 2, (i % 2) * 8:(i % 2) * 8 + 8] = packs[i]
        for i in range(2):
            packed = jnp.zeros((8, 128), f32)
            for r in range(16):
                row = jnp.broadcast_to(planes[3, r:r + 1, (1 - i) * 128:(1 - i) * 128 + 128], (8, 128))
                packed = jnp.where(half == r, roll(row, 2 * r + 2 * (1 - i), 1), packed)
            tpack[i, 16:24] = spread_groups(packed)

    def spread_groups(x):
        x = jnp.where(lane < 32, x, 0.0)
        x = x + roll(x, 32, 1)
        return x + roll(x, 64, 1)

    two = (slice(None), slice(0, 256))
    level = subs((8, 256)).astype(f32)

    def own_row(ref, r):
        return jnp.concatenate([jnp.broadcast_to(ref[b, pl.ds(r, 1), :], (8, 128)) for b in range(2)], axis=1)

    def start_flow(dst, src, r, rn):
        mn = own_row(mn_r, r)
        for q in range(8):
            part = slice(q * 8, q * 8 + 8)
            dst[part] = jnp.where(level + float(q * 8) < mn, src[rn, part] - src[r, part], 0.0)

    def lap_row(r, _):
        rn = lax.rem(r + 1, 24)
        me, mn = own_row(mc_r, r), own_row(mn_r, r)
        for q in range(8):
            part = slice(q * 8, q * 8 + 8)
            lev = level + float(q * 8)
            t = tv[r, part]
            fe = jnp.where(lev < me, east(t) - t, 0.0)
            fn = jnp.where(lev < mn, tv[rn, part] - t, 0.0)
            lap[r, part] = fe - west(fe) + fn - flow[part]
            flow[part] = fn
        return 0

    def mix_row(r, _):
        me, mn = own_row(mc_r, r), own_row(mn_r, r)
        for q in range(8):
            part = slice(q * 8, q * 8 + 8)
            lev = level + float(q * 8)
            t = lap[r, part]
            fe = jnp.where(lev < me, east(t) - t, 0.0)
            fn = jnp.where(lev < mn, lap[r + 1, part] - t, 0.0)
            mix[r, part] = (-mixing_fourth) * (fe - west(fe) + fn - flow2[part])
            flow2[part] = fn
        return 0

    def sum_north(r, rn):
        mn = own_row(mn_r, r)
        for q in range(8):
            part = slice(q * 8, q * 8 + 8)
            both = tv[r, part] + tv[rn, part]
            face_n[r, part] = jnp.where(level + float(q * 8) < mn, both, 0.0)

    def sum_east(r):
        me = own_row(mc_r, r)
        for q in range(8):
            part = slice(q * 8, q * 8 + 8)
            t = tv[r, part]
            face_e[r, part] = jnp.where(level + float(q * 8) < me, t + east(t), 0.0)

    def sum_row(r, _):
        sum_east(r)
        sum_north(r, r + 1)
        return 0

    def do_inner():
        start_flow(flow, tv, 0, 1)
        lax.fori_loop(1, 15, lap_row, 0)
        start_flow(flow2, lap, 1, 2)
        lax.fori_loop(2, 14, mix_row, 0)
        lax.fori_loop(0, 15, sum_row, 0)
        sum_east(15)

    def do_vertical():
        def vertical(i, below):
            below = list(below)
            for j in range(4):
                l = i * 4 + j
                lev = l.astype(f32)
                for rt in range(2):
                    for b in range(2):
                        c = planes[3, rt * 8:rt * 8 + 8, b * 128:b * 128 + 128]
                        at = pl.multiple_of(l * 16 + rt * 8, 8)
                        t = tn[b, pl.ds(at, 8)]
                        up = tn[b, pl.ds(pl.multiple_of(lax.rem(at + 16, 1024), 8), 8)]
                        down = jnp.where(lev + 1.0 < c, up - t, 0.0)
                        gain = diapycnal_diffusion * (down - below[rt * 2 + b])
                        tpart[b, pl.ds(at, 8)] = t + jnp.where(lev < c, gain, 0.0)
                        below[rt * 2 + b] = down
            return tuple(below)

        lax.fori_loop(0, strata // 4, vertical, (jnp.zeros((8, 128), f32),) * 4)

    c_own = planes[3]
    c_east = jnp.where(lanes((16, 256)) == 255, 0.0, jnp.minimum(c_own, east(c_own)))
    c_north = jnp.minimum(c_own, north(c_own))
    for b in range(2):
        mc_r[b, 0:16] = c_east[:, b * 128:b * 128 + 128]
        mn_r[b, 0:16] = c_north[:, b * 128:b * 128 + 128]

    early = lax.rem(lon, n_lon // 2) < n_lon // 4

    @pl.when(early)
    def _():
        do_turn()
        do_vertical()
        do_inner()

    pl.semaphore_wait(barrier, 2 + 3 * has_n.astype(jnp.int32) + 3 * has_s.astype(jnp.int32))

    x_copies = [plan(masked, rx.at[0], to_n), plan(masked, rx.at[1], to_s)]
    start(x_copies)
    p_copies = [
        plan(col_e, rcol_w, to_e),
        plan(col_w, rcol_e, to_w),
        plan(col_e.at[pl.ds(8, 8)], rdiag.at[3], to_ne),
        plan(col_w.at[pl.ds(8, 8)], rdiag.at[2], to_nw),
        plan(col_e.at[pl.ds(0, 8)], rdiag.at[1], to_se),
        plan(col_w.at[pl.ds(0, 8)], rdiag.at[0], to_sw),
        plan(planes.at[:, pl.ds(8, 8)], rns.at[1], to_n),
        plan(planes.at[:, pl.ds(0, 8)], rns.at[0], to_s),
    ]
    start(p_copies)

    load[11].wait()
    for j in range(8):
        rows_wide[j:j + 1, 0:16] = rows_in[j // 2, j % 2:j % 2 + 1, :].astype(f32)
    row_of = jnp.zeros((8, 128), f32)
    for j in range(8):
        here = lax.shift_right_logical(lane, 4) == j
        row_of = jnp.where(here, roll(jnp.broadcast_to(rows_wide[j:j + 1, :], (8, 128)), 16 * j, 1), row_of)
    row_id = subs((128, 128))
    hot = (row_id & 31).astype(f32) == jnp.concatenate([row_of] * 16, axis=0)
    hot = jnp.where(hot & (row_id < 96), 1.0, 0.0)
    row_hot[...] = hot[0:32].astype(bf16)
    rowcol[...] = jnp.transpose(hot).astype(bf16)

    @pl.when(jnp.logical_not(early))
    def _():
        do_turn()

    t_copies = [
        plan(tpack.at[0], rt_w, to_e),
        plan(tpack.at[1], rt_e, to_w),
        plan(tpack.at[0], rt_diag.at[3], to_ne),
        plan(tpack.at[1], rt_diag.at[2], to_nw),
        plan(tpack.at[0], rt_diag.at[1], to_se),
        plan(tpack.at[1], rt_diag.at[0], to_sw),
        plan(tv.at[pl.ds(14, 2)], tv.at[pl.ds(22, 2)], to_n),
        plan(tv.at[pl.ds(0, 2)], tv.at[pl.ds(16, 2)], to_s),
        plan(tpack, rt_ns.at[1], to_n),
        plan(tpack, rt_ns.at[0], to_s),
    ]
    start(t_copies)

    for i in range(7, 11):
        load[i].wait()

    arrive(x_copies)
    keep_south = jnp.broadcast_to(lat, (8, 128)) > 0
    keep_north = jnp.broadcast_to(lat, (8, 128)) < n_lat - 1
    zero = jnp.zeros((8, 128), f32)
    def regrid(f):
        part = slice(f * 8, f * 8 + 8)
        bands = jnp.concatenate(
            [jnp.where(keep_south, rx[0, part], 0.0), masked[part], jnp.where(keep_north, rx[1, part], 0.0), zero], axis=0
        )
        high = bands.astype(bf16)
        rest = bands - high.astype(f32)
        mid = rest.astype(bf16)
        low = (rest - mid.astype(f32)).astype(bf16)
        picked = jnp.dot(
            rowcol[...], jnp.concatenate([high, mid, low, jnp.zeros((32, 128), bf16)], axis=0), preferred_element_type=f32
        )
        for b in range(2):
            for rt in range(2):
                acc = zero
                for k in range(4):
                    m = (k * 2 + b) * 16 + rt * 8
                    at = slice(k * 16 + rt * 8, k * 16 + rt * 8 + 8)
                    cell = jnp.take_along_axis(picked[m:m + 8], pt[b, at], axis=1, mode="promise_in_bounds")
                    acc = acc + cell * wt[b, at]
                forcing[b, rt * 64 + f * 8:rt * 64 + f * 8 + 8] = acc

    for f in range(3):
        regrid(f)

    def forcing_tile(f, rt, b):
        return forcing[b, rt * 64 + f * 8:rt * 64 + f * 8 + 8]

    pack_columns(forcing_tile, 3, fcol_e, fcol_w)

    f_copies = [
        plan(fcol_e, rf_w, to_e),
        plan(fcol_w, rf_e, to_w),
        plan(fcol_e.at[pl.ds(8, 8)], rf_diag.at[3], to_ne),
        plan(fcol_w.at[pl.ds(8, 8)], rf_diag.at[2], to_nw),
        plan(fcol_e.at[pl.ds(0, 8)], rf_diag.at[1], to_se),
        plan(fcol_w.at[pl.ds(0, 8)], rf_diag.at[0], to_sw),
        plan(forcing.at[:, pl.ds(64, 24)], rf_ns.at[1], to_n),
        plan(forcing.at[:, pl.ds(0, 24)], rf_ns.at[0], to_s),
    ]
    start(f_copies)

    for f in range(3, 5):
        regrid(f)

    def extended(p, tiles, ns, ce, cw, diag):
        def side(e, w):
            return jnp.where(lane < 64, roll(e, -3 * p, 1), roll(w, 125 - 3 * p, 1))

        rows = []
        for rt in range(2):
            part = slice(rt * 8, rt * 8 + 8)
            rows.append(jnp.concatenate([tiles(p, rt, 0), tiles(p, rt, 1), side(ce[part], cw[part])], axis=1))
        def rim(north_side, south_side):
            return jnp.where(sub < 4, jnp.where(keep_north, north_side, 0.0), jnp.where(keep_south, south_side, 0.0))

        edge = [rim(ns(0, p, b), ns(1, p, b)) for b in range(2)]
        corner = rim(side(diag[0], diag[1]), side(diag[2], diag[3]))
        rows.append(jnp.concatenate(edge + [corner], axis=1))
        return jnp.concatenate(rows, axis=0)

    arrive(p_copies)

    def plane_ns(i, p, b):
        return rns[i, p, :, b * 128:b * 128 + 128]

    height, zonal, meridional, count, top = [
        extended(p, plane_tile, plane_ns, rcol_e, rcol_w, rdiag) for p in range(5)
    ]
    row_ids = subs((24, 384))
    off_grid = ((lat == n_lat - 1) & (row_ids >= 16) & (row_ids < 20)) | ((lat == 0) & (row_ids >= 20))
    count = jnp.where(off_grid, 0.0, count)

    scale = 1.0 / (2.0 * strata)

    def depth(c):
        return c * scale + c * (c - 1.0) * (scale / strata)

    min_e = jnp.minimum(count, east(count))
    min_n = jnp.minimum(count, north(count))
    put(cnt_r, count)
    put(me_r, min_e)
    put(mn_r, min_n)
    closed = jnp.where(lanes((24, 384)) == 255, 0.0, min_e)
    for b in range(2):
        mc_r[b] = closed[:, b * 128:b * 128 + 128]

    def plane_laplace(field):
        fe = jnp.where(whole(me_r) > 0.5, east(field) - field, 0.0)
        fn = jnp.where(whole(mn_r) > 0.5, north(field) - field, 0.0)
        return fe - west(fe) + fn - south(fn)

    wet_own = (own_part(cnt_r) > 0.5).astype(f32)
    top_mix = plane_laplace(plane_laplace(top))[0:16, 0:256]

    def own_forcing(f):
        return jnp.concatenate(
            [jnp.concatenate([forcing_tile(f, rt, 0), forcing_tile(f, rt, 1)], axis=1) for rt in range(2)], axis=0
        )

    heat, light = own_forcing(3), own_forcing(4)
    for b in range(2):
        light_r[b] = (light_gain * absorb_of) * light[:, b * 128:b * 128 + 128]
    t_own = planes[4]
    t_next = jnp.concatenate([tn[0, 16:32], tn[1, 16:32]], axis=1)
    top_part[...] = (
        t_own
        + wet_own
        * (
            diapycnal_diffusion * jnp.where(own_part(cnt_r) > 1.5, t_next - t_own, 0.0)
            + light_gain * absorb_of * light
            + heat_gain * heat
        )
        - mixing_fourth * top_mix
    )

    arrive(t_copies)

    @pl.when(jnp.logical_not(early))
    def _():
        do_inner()
        do_vertical()

    lax.fori_loop(15, 17, lap_row, 0)
    start_flow(flow, tv, 22, 23)
    lax.fori_loop(0, 2, lambda i, _: lap_row(lax.rem(i + 23, 24), 0), 0)
    lax.fori_loop(14, 16, mix_row, 0)
    start_flow(flow2, lap, 23, 0)
    lax.fori_loop(0, 2, mix_row, 0)
    sum_north(15, 16)
    sum_north(23, 0)

    fade = jnp.exp(-level / light_decay)

    def source_row(r, _):
        cnt, light = own_row(cnt_r, r), own_row(light_r, r) * fade
        for q in range(8):
            part = slice(q * 8, q * 8 + 8)
            lit = light * math.exp(-q * 8 / light_decay)
            mix[r, part] = mix[r, part] + jnp.where(level + float(q * 8) < cnt, lit, 0.0)
        return 0

    lax.fori_loop(0, 16, source_row, 0)

    odd = (lane & 1) == 1
    group_lane = lane & 31
    keep_s, keep_n = keep_south, keep_north

    def edge(side):
        beside = rt_e if side == 0 else rt_w
        diag_n, diag_s = (rt_diag.at[0], rt_diag.at[2]) if side == 0 else (rt_diag.at[1], rt_diag.at[3])

        def join(own_pack, other):
            return jnp.where(odd, own_pack, other) if side == 0 else jnp.where(odd, other, own_pack)

        def shift_out(own_pack, other):
            return jnp.where(odd, roll(other, 1, 1), roll(other, -1, 1)) if side == 0 else jnp.where(
                odd, roll(other, 1, 1), roll(other, -1, 1)
            )

        def shift_in(own_pack, other):
            return jnp.where(odd, roll(own_pack, 1, 1), roll(own_pack, -1, 1))

        def up(x, x_n):
            return jnp.where(group_lane >= 30, roll(x_n, 30, 1), roll(x, -2, 1))

        def down(x, x_s):
            return jnp.where(group_lane < 2, roll(x_s, -30, 1), roll(x, 2, 1))

        mine = jnp.logical_not(odd) if side == 1 else odd
        back = 1 if side == 0 else -1
        rows = slice(16, 24)
        c = join(tpack[side, rows], beside[rows])
        c_out, c_in = shift_out(tpack[side, rows], beside[rows]), shift_in(tpack[side, rows], beside[rows])
        cn_pack = jnp.where(keep_n, join(rt_ns[0, side, rows], diag_n[rows]), 0.0)
        cs_pack = jnp.where(keep_s, join(rt_ns[1, side, rows], diag_s[rows]), 0.0)
        cn_out = jnp.where(keep_n, shift_out(rt_ns[0, side, rows], diag_n[rows]), 0.0)
        cs_out = jnp.where(keep_s, shift_out(rt_ns[1, side, rows], diag_s[rows]), 0.0)
        m_out, m_in = jnp.minimum(c, c_out), jnp.minimum(c, c_in)
        m_n, m_s = jnp.minimum(c, up(c, cn_pack)), jnp.minimum(c, down(c, cs_pack))
        m_n_out, m_s_out = jnp.minimum(cn_pack, cn_out), jnp.minimum(cs_pack, cs_out)
        for g in range(2):
            part = slice(g * 8, g * 8 + 8)
            lev = (sub + 8 * (4 * g + lax.shift_right_logical(lane, 5))).astype(f32)
            own_pack, other = tpack[side, part], beside[part]
            own_n, other_n = rt_ns[0, side, part], diag_n[part]
            own_s, other_s = rt_ns[1, side, part], diag_s[part]
            z = join(own_pack, other)
            z_n, z_s = join(own_n, other_n), join(own_s, other_s)
            z_out = shift_out(own_pack, other)
            flux_out = jnp.where(lev < m_out, z_out - z, 0.0)
            flux_in = jnp.where(lev < m_in, shift_in(own_pack, other) - z, 0.0)
            flux_n = jnp.where(lev < m_n, up(z, z_n) - z, 0.0)
            flux_s = jnp.where(lev < m_s, down(z, z_s) - z, 0.0)
            full = flux_out + flux_in + flux_n + flux_s
            missing = jnp.where(mine, flux_out, 0.0)
            missing_n = jnp.where(lev < m_n_out, shift_out(own_n, other_n) - z_n, 0.0)
            missing_s = jnp.where(lev < m_s_out, shift_out(own_s, other_s) - z_s, 0.0)
            inward = jnp.where(lev < m_in, missing, 0.0)
            change = (
                jnp.where(lev < m_out, roll(full, back, 1) - full, 0.0)
                - inward
                + jnp.where(lev < m_n, up(missing, missing_n) - missing, 0.0)
                + jnp.where(lev < m_s, down(missing, missing_s) - missing, 0.0)
            )
            change = jnp.where(mine, change, roll(inward, -back, 1))
            edge_mix[side, part] = (-mixing_fourth) * change
            edge_sum[side, part] = jnp.where(mine & (lev < m_out), z_out + z, 0.0)

    edge(0)
    edge(1)

    leave(x_copies + p_copies + t_copies)
    arrive(f_copies)

    def forcing_ns(i, f, b):
        return rf_ns[i, b, f * 8:f * 8 + 8]

    wind_e, wind_n, fresh = [
        extended(f, forcing_tile, forcing_ns, rf_e, rf_w, rf_diag) for f in range(3)
    ]
    min_e, min_n = whole(me_r), whole(mn_r)
    depth_e, depth_n = depth(min_e), depth(min_n)
    pull_e, pull_n = grav_step * depth_e, grav_step * depth_n
    push_e = jnp.where(min_e > 0.5, wind_step * wind_e, 0.0)
    push_n = jnp.where(min_n > 0.5, wind_step * wind_n, 0.0)
    gain = jnp.where(whole(cnt_r) > 0.5, fresh_step * fresh, 0.0)
    zonal = jnp.where(min_e > 0.5, zonal, 0.0)
    meridional = jnp.where(min_n > 0.5, meridional, 0.0)
    for _ in range(SUBS):
        zonal = zonal - pull_e * (east(height) - height) + push_e
        meridional = meridional - pull_n * (north(height) - height) + push_n
        height = height + gain - height_step * (zonal - west(zonal) + meridional - south(meridional))

    own = (slice(0, 16), slice(0, 256))
    o_height[...] = height[own]
    o_zonal[...] = zonal[own]
    o_meridional[...] = meridional[own]
    speed_e = zonal * ((-0.5 * advect_coef) / jnp.maximum(depth_e, depth_floor))
    speed_n = meridional * ((-0.5 * advect_coef) / jnp.maximum(depth_n, depth_floor))
    put(se_r, speed_e)
    put(sn_r, speed_n)

    ce = speed_e * (top + east(top))
    cn = speed_n * (top + north(top))
    top_new = top_part[...] + (ce - west(ce) + cn - south(cn))[own]
    inverse = wet_own / jnp.maximum(depth(own_part(cnt_r)), depth_floor)
    surface = [top_new * wet_own, height[own] * wet_own, zonal[own] * inverse, meridional[own] * inverse, wet_own]
    for s in range(8):
        for b in range(2):
            piece = surface[s][:, b * 128:b * 128 + 128] if s < 5 else jnp.zeros((16, 128), f32)
            sv[pl.ds(b * 8 + s, 16, stride=16), :] = piece

    cell_id = lax.broadcasted_iota(jnp.int32, (128, 128), 0).astype(f32).astype(bf16)

    wide_id = jnp.concatenate([cell_id, cell_id], axis=1)
    blank = jnp.zeros((16, 128), bf16)

    def spread(r, _):
        value = sv[pl.ds(pl.multiple_of(r * 16, 16), 16), :]
        for k in range(4):
            parts, points = [], []
            for b in range(2):
                share = value[b * 8:b * 8 + 8] * wt[b, pl.ds(k * 16 + r, 1), :]
                high = share.astype(bf16)
                low = (share - high.astype(f32)).astype(bf16)
                parts.append(jnp.concatenate([high, low], axis=0))
                points.append(pt[b, pl.ds(k * 16 + r, 1), :].astype(f32).astype(bf16))
            left = jnp.concatenate(
                [jnp.concatenate([parts[0], blank], axis=1), jnp.concatenate([blank, parts[1]], axis=1)], axis=0
            )
            match = jnp.where(wide_id == jnp.concatenate(points, axis=1), bf16(1), bf16(0))
            by_cell = lax.dot_general(left, match, (((1,), (1,)), ((), ())), preferred_element_type=f32)
            for b in range(2):
                both = by_cell[b * 16:b * 16 + 8] + by_cell[b * 16 + 8:b * 16 + 16]
                cells[pl.ds((k * 2 + b) * 16 + r, 8, stride=128), :] = both
        return 0

    lax.fori_loop(0, 16, spread, 0, unroll=2)

    for s in range(5):
        part = cells[s * 128:s * 128 + 128]
        high = part.astype(bf16)
        low = (part - high.astype(f32)).astype(bf16)
        rows = jnp.dot(row_hot[...], high, preferred_element_type=f32) + jnp.dot(
            row_hot[...], low, preferred_element_type=f32
        )
        for band in range(3):
            table[band, s * 8:s * 8 + 8] = rows[band * 8:band * 8 + 8]

    s_copies = [plan(table.at[0], rtable.at[1], to_s), plan(table.at[2], rtable.at[0], to_n)]
    start(s_copies)

    for side in range(2):
        lane_of = (lane & 1) == 1 if side == 0 else (lane & 1) == 0
        packed = zero
        for r in range(16):
            row = jnp.broadcast_to(se_r[1 + side, r:r + 1, :], (8, 128))
            here = lane == 2 * r + 1 - side
            packed = jnp.where(here, roll(row, 2 * r + 1 - side - 127, 1), packed)
        speed = spread_groups(packed)
        sign = 1.0 if side == 0 else -1.0
        for g in range(2):
            part = slice(g * 8, g * 8 + 8)
            total = edge_mix[side, part] + sign * speed * edge_sum[side, part]
            for q4 in range(4):
                q = g * 4 + q4
                edge_all[side, q * 8:q * 8 + 8] = roll(total, -32 * q4 - 2 * (1 - side), 1)

    vn = own_row(sn_r, 23)
    for q in range(8):
        part = slice(q * 8, q * 8 + 8)
        flow[part] = vn * face_n[23, part]

    def advect_row(r, _):
        ve, vn = own_row(se_r, r), own_row(sn_r, r)
        turn_by = (128 - 2 * r) & 127
        for q in range(8):
            part = slice(q * 8, q * 8 + 8)
            fe, fn = ve * face_e[r, part], vn * face_n[r, part]
            change = mix[r, part] + (fe - west(fe)) + (fn - flow[part])
            flow[part] = fn
            edge_w = jnp.where(lane < 2, pltpu.roll(edge_all[1, part], turn_by, 1), 0.0)
            edge_e = jnp.where(lane >= 126, pltpu.roll(edge_all[0, part], turn_by, 1), 0.0)
            at = pl.ds(q * 128 + r, 8, stride=16)
            tnew[0, at, :] = tpart[0, at, :] + (change[:, 0:128] + edge_w)
            tnew[1, at, :] = tpart[1, at, :] + (change[:, 128:256] + edge_e)
        return 0

    lax.fori_loop(0, 16, advect_row, 0)
    for rt in range(2):
        rows = slice(rt * 8, rt * 8 + 8)
        for b in range(2):
            tnew[b, rows] = tnew[b, rows] + jnp.where(
                cnt_r[b, rows] > 0.5, heat_gain * forcing[b, rt * 64 + 24:rt * 64 + 32], 0.0
            )

    leave(f_copies)
    arrive(s_copies)

    def from_bands(s):
        part = slice(s * 8, s * 8 + 8)
        from_south = jnp.where(keep_south, rtable[0, part], 0.0)
        from_north = jnp.where(keep_north, rtable[1, part], 0.0)
        return table[1, part] + from_south + from_north

    factor = (1 - flags[...]).astype(f32) / jnp.maximum(from_bands(4), area_floor)
    for s in range(4):
        o_skin[s * 8:s * 8 + 8] = from_bands(s) * factor
    leave(s_copies)


def deliver(height, zonal, meridional, thermal, skin, h_out, u_out, v_out, t_out, skin_out, sem):
    rows = t_out.shape[0]
    copies = [(height, h_out), (zonal, u_out), (meridional, v_out), (skin, skin_out)]
    copies += [(thermal.at[b, pl.ds(0, rows)], t_out.at[:, pl.ds(b * 128, 128)]) for b in range(2)]
    copies = [pltpu.make_async_copy(a, b, sem.at[i]) for i, (a, b) in enumerate(copies)]
    for c in copies:
        c.start()
    for c in copies:
        c.wait()


def shards(
    free_elevation, zonal_volume_carriage, meridional_volume_carriage, thermal_field, flooded_strata_number,
    aerial_exchanges, aerial_terrain_flags, donor_tile_number, donor_point_number, pairing_coefficients,
):
    strata = thermal_field.shape[0]
    vmem = pltpu.VMEM
    anywhere = pl.BlockSpec(memory_space=pl.ANY)
    far = pl.BlockSpec(memory_space=pltpu.HBM)
    local = pl.BlockSpec(memory_space=pltpu.VMEM)
    results = pl.pallas_call(
        kernel,
        out_shape=(vmem((16, 256), f32),) * 3 + (vmem((2, 1024, 128), f32), vmem((32, 128), f32)),
        in_specs=[far] * 10,
        out_specs=(local,) * 5,
        scratch_shapes=[
            vmem((5, 16, 256), f32), vmem((16, 256), jnp.int32), vmem((2, 1024, 128), f32), vmem((40, 128), f32),
            vmem((8, 128), jnp.int32), vmem((2, 64, 128), jnp.int32), vmem((2, 64, 128), f32),
            vmem((4, 2, 16), jnp.int32), vmem((8, 128), f32), vmem((40, 128), f32), vmem((2, 40, 128), f32),
            vmem((16, 128), f32), vmem((16, 128), f32), vmem((16, 128), f32), vmem((16, 128), f32),
            vmem((4, 8, 128), f32), vmem((2, 5, 8, 256), f32),
            vmem((24, 64, 256), f32), vmem((2, 24, 128), f32), vmem((24, 128), f32), vmem((24, 128), f32),
            vmem((4, 24, 128), f32), vmem((2, 2, 24, 128), f32), vmem((2, 16, 128), f32), vmem((2, 16, 128), f32),
            vmem((2, 64, 128), f32),
            vmem((2, 128, 128), f32), vmem((16, 128), f32), vmem((16, 128), f32), vmem((16, 128), f32),
            vmem((16, 128), f32), vmem((4, 8, 128), f32), vmem((2, 2, 24, 128), f32),
            vmem((3, 24, 128), f32), vmem((3, 24, 128), f32), vmem((3, 24, 128), f32), vmem((3, 24, 128), f32),
            vmem((3, 24, 128), f32), vmem((2, 24, 128), f32), vmem((2, 16, 128), f32),
            vmem((24, 64, 256), f32), vmem((16, 64, 256), f32), vmem((2, 1024, 128), f32), vmem((64, 256), f32), vmem((64, 256), f32),
            vmem((16, 64, 256), f32), vmem((24, 64, 256), f32),
            vmem((128, 128), bf16), vmem((32, 128), bf16), vmem((256, 128), f32), vmem((1024, 128), f32),
            vmem((3, 40, 128), f32), vmem((2, 40, 128), f32), vmem((16, 256), f32),
            pltpu.SemaphoreType.DMA((14,)),
            pltpu.SemaphoreType.DMA((30,)), pltpu.SemaphoreType.DMA((30,)),
        ],
        compiler_params=pltpu.CompilerParams(collective_id=0, has_side_effects=True, vmem_limit_bytes=65929216),
    )(
        free_elevation, zonal_volume_carriage, meridional_volume_carriage, thermal_field.reshape(strata * 16, 256),
        flooded_strata_number, aerial_exchanges.reshape(40, 128), aerial_terrain_flags, donor_tile_number.swapaxes(1, 2),
        donor_point_number.reshape(64, 256), pairing_coefficients.reshape(64, 256),
    )
    plane = jax.ShapeDtypeStruct((16, 256), f32)
    h, u, v, t, skin = pl.pallas_call(
        deliver,
        out_shape=(plane,) * 3 + (jax.ShapeDtypeStruct((strata * 16, 256), f32), jax.ShapeDtypeStruct((32, 128), f32)),
        in_specs=[local] * 5,
        out_specs=(anywhere,) * 5,
        scratch_shapes=[pltpu.SemaphoreType.DMA((6,))],
        compiler_params=pltpu.CompilerParams(vmem_limit_bytes=8 << 20),
    )(*results)
    return h, u, v, t.reshape(strata, 16, 256), skin.reshape(4, 8, 128)


def solution(mesh):
    flat, deep = P("lat", "lon"), P(None, "lat", "lon")
    return jax.shard_map(
        shards,
        mesh=mesh,
        in_specs=(flat, flat, flat, deep, flat, deep, flat, deep, deep, deep),
        out_specs=(flat, flat, flat, deep, deep),
        check_vma=False,
    )
```
